32 devices in a mesh: energy: 8 (over z, y), section: 4 (over x, core).
Axes of the slice: x: 2, y: 2, z: 4, core: 2. Of those that a mesh axis runs over, the one named last changes fastest.
Arguments:
- onsite: float32 [8, 256], P('section'), may hold values from -1 to 1
- hopping: float32 [8, 256, 256], P('section'), may hold values from -0.125 to 0.125
- coupling: float32 [8, 256, 256], P('section'), may hold values from -4 to 4
- broadening: float32 [8], P('energy'), may hold values from 1.5 to 3
- born_sigma: float32 [8, 8, 2, 256, 256], P('energy', 'section'), may hold values from -0.046875 to 0.046875
- phonon_shift: int32 [4], replicated, may hold values from -2 to 2
- phonon_local: float32 [4, 256, 256], replicated, may hold values from 0.5 to 4
- phonon_side: float32 [4, 256, 256], replicated, may hold values from 0.2 to 2
Outputs:
- next_sigma: float32 [8, 8, 2, 256, 256], P('energy', 'section')
The draws below stay inside these ranges and needn't reach their ends.
All inputs are finite; a program needn't handle non-finite values.
Results may differ from the reference program's by a relative error of at most 0.0001.
Values sent between devices are 32-bit elements; how exact they have to be, the bound alone decides.
No kernel may reach another device: no remote copies, remote signals or barrier semaphores. Data moves between devices by JAX's collectives and lax.ppermute only.
A program may use at most 128 MiB of HBM per device.

```python
import math
import jax
import jax.numpy as jnp
from jax import lax

B = 256
MODES = 4
NS_ITERS = 3
OMAX = 2
NE = 8
NB = 8


def draw_coupling(key, part):
    base = jax.random.fold_in(key, 7)
    key_sign, key_size, key_dense = jax.random.split(base, 3)
    magnitude = jax.random.uniform(key_size, (NB, B), jnp.float32, 2.5, 3.5)
    spread = 1.0 / math.sqrt(8.0 * B)
    dense = jax.random.truncated_normal(key_dense, -6.0, 6.0, (NB, B, B), jnp.float32) * spread
    flips = jax.random.bernoulli(key_sign, 0.5, (NB, B))
    signed = jnp.where(flips, 1.0, -1.0).astype(jnp.float32) * magnitude
    diagonal = signed[:, :, None] * jnp.eye(B, dtype=jnp.float32)[None]
    return (diagonal + dense).astype(jnp.float32)


def place_ends(entries, key, low, top_value):
    longest = entries.shape.index(max(entries.shape))
    spots = []
    for shift in (0, 1):
        where = [jax.random.randint(jax.random.fold_in(key, axis), (), 0, length) for axis, length in enumerate(entries.shape)]
        where[longest] = (where[longest] + shift) % entries.shape[longest]
        spots.append(tuple(where))
    return entries.at[spots[0]].set(low).at[spots[1]].set(top_value)


def block_levels(key, extent, cuts, smallest, top_value):
    def one(dim, shards_of):
        steps = jax.random.uniform(jax.random.fold_in(jax.random.fold_in(key, 6), dim), (shards_of,), jnp.float32, smallest / len(cuts), top_value / len(cuts))
        return jnp.repeat(jnp.exp(steps), extent[dim] // shards_of).reshape((-1,) + (1,) * (len(extent) - dim - 1))

    gain = one(*cuts[0])
    for cut in cuts[1:]:
        gain = gain * one(*cut)
    return gain


def centred(rng, dims, scale, most, pieces=(), held_as=jnp.bfloat16):
    level = block_levels(rng, dims, pieces, -0.22, 0.18) if pieces else 1.0
    values = jax.random.normal(rng, dims, jnp.float32) * scale * level
    return jnp.minimum(jnp.maximum(values, -most), most).astype(held_as)


def setup_inputs(seed: int = 0) -> dict:
    streams_of = jax.random.split(jax.random.key(seed), 9)
    onsite = jnp.clip(jax.random.uniform(streams_of[0], (NB, B), jnp.float32, -1.0, 1.0) * block_levels(streams_of[0], (NB, B), ((0, 4),), -0.4, 0.0), -1.0, 1.0)
    hopping = centred(streams_of[1], (NB, B, B), (8 * B) ** -0.5, 0.125, ((0, 4),), jnp.float32)
    coupling = draw_coupling(jax.random.fold_in(streams_of[8], 71), 0)
    broadening = jnp.clip(jnp.exp(math.log(3.0) - 0.6931472 * jax.random.uniform(streams_of[3], (NE,), jnp.float32) ** block_levels(streams_of[3], (NE,), ((0, 8),), -0.2, 0.2)), 1.5, 3.0)
    born_sigma = centred(streams_of[4], (NE, NB, 2, B, B), (64 * B) ** -0.5, 0.046875, ((0, 8), (1, 4)), jnp.float32)
    phonon_shift = place_ends(jax.random.randint(streams_of[5], (MODES,), -OMAX, OMAX + 1), jax.random.fold_in(streams_of[5], 1), -OMAX, OMAX).astype(jnp.int32)
    phonon_local = jnp.clip(jnp.exp(jax.random.uniform(streams_of[6], (MODES, B, B), jnp.float32, math.log(0.5), math.log(4.0))), 0.5, 4.0)
    phonon_side = jnp.clip(jnp.exp(jax.random.uniform(streams_of[7], (MODES, B, B), jnp.float32, math.log(0.2), math.log(2.0))), 0.2, 2.0)
    return {"onsite": onsite, "hopping": hopping, "coupling": coupling, "broadening": broadening, "born_sigma": born_sigma, "phonon_shift": phonon_shift, "phonon_local": phonon_local, "phonon_side": phonon_side}


HIGH = lax.Precision.HIGHEST


def matmul(left, right):
    return jnp.matmul(left, right, precision=HIGH)


def complex_product(left, right):
    left_real = left[..., 0, :, :]
    left_imag = left[..., 1, :, :]
    right_real = right[..., 0, :, :]
    right_imag = right[..., 1, :, :]
    return jnp.stack([matmul(left_real, right_real) - matmul(left_imag, right_imag),
                      matmul(left_real, right_imag) + matmul(left_imag, right_real)], axis=-3)


def newton_inverse(matrix):
    dimension = matrix.shape[-1]
    identity = jnp.eye(dimension, dtype=jnp.float32)
    mat_real = matrix[..., 0, :, :]
    mat_imag = matrix[..., 1, :, :]
    diag_real = jnp.diagonal(mat_real, axis1=-2, axis2=-1)
    diag_imag = jnp.diagonal(mat_imag, axis1=-2, axis2=-1)
    modulus = diag_real * diag_real + diag_imag * diag_imag
    inv_real = diag_real / modulus
    inv_imag = -diag_imag / modulus
    col_real = inv_real[..., None, :]
    col_imag = inv_imag[..., None, :]
    scaled_real = mat_real * col_real - mat_imag * col_imag
    scaled_imag = mat_real * col_imag + mat_imag * col_real
    remain_real = 2.0 * identity - scaled_real
    remain_imag = -scaled_imag
    row_real = inv_real[..., :, None]
    row_imag = inv_imag[..., :, None]
    current = jnp.stack([row_real * remain_real - row_imag * remain_imag,
                         row_real * remain_imag + row_imag * remain_real], axis=-3)
    for repeat in range(NS_ITERS - 1):
        product = complex_product(matrix, current)
        remainder = jnp.stack([2.0 * identity - product[..., 0, :, :], -product[..., 1, :, :]], axis=-3)
        current = complex_product(current, remainder)
    return current


def left_couple(link, green_block):
    transposed = jnp.swapaxes(link, -1, -2)[..., None, :, :]
    return matmul(matmul(transposed, green_block), link[..., None, :, :])


def right_couple(link, green_block):
    transposed = jnp.swapaxes(link, -1, -2)[..., None, :, :]
    return matmul(matmul(link[..., None, :, :], green_block), transposed)


def reference(onsite, hopping, coupling, broadening, born_sigma, phonon_shift, phonon_local, phonon_side):
    dimension = onsite.shape[1]
    block_count = onsite.shape[0]
    identity = jnp.eye(dimension, dtype=jnp.float32)
    hamiltonian = 0.5 * (hopping + jnp.swapaxes(hopping, -1, -2)) + onsite[:, :, None] * identity
    energy_values = -2.0 + 4.0 * jnp.arange(NE, dtype=jnp.float32) / (NE - 1)
    sys_real = energy_values[:, None, None, None] * identity - hamiltonian[None] - born_sigma[:, :, 0]
    sys_imag = broadening[:, None, None, None] * identity - born_sigma[:, :, 1]
    system = jnp.stack([sys_real, sys_imag], axis=2)
    incoming = jnp.zeros((NE, 2, dimension, dimension), jnp.float32)
    left_sigma = []
    for block_index in range(block_count):
        left_sigma.append(incoming)
        green_left = newton_inverse(system[:, block_index] - incoming)
        incoming = left_couple(coupling[block_index], green_left)
    arriving = jnp.zeros((NE, 2, dimension, dimension), jnp.float32)
    right_sigma = [None] * block_count
    for block_index in range(block_count - 1, -1, -1):
        self_energy = right_couple(coupling[block_index], arriving)
        right_sigma[block_index] = self_energy
        arriving = newton_inverse(system[:, block_index] - self_energy)
    green_list = []
    for block_index in range(block_count):
        green_list.append(newton_inverse((system[:, block_index] - left_sigma[block_index]) - right_sigma[block_index]))
    green = jnp.stack(green_list, axis=1)
    padded = jnp.pad(green, ((OMAX, OMAX), (0, 0), (0, 0), (0, 0), (0, 0)))
    local_sum = jnp.zeros(green.shape, jnp.float32)
    side_sum = jnp.zeros(green.shape, jnp.float32)
    for mode_index in range(MODES):
        begin = (phonon_shift[mode_index] + OMAX).astype(jnp.int32)
        shifted = lax.dynamic_slice_in_dim(padded, begin, NE, 0)
        local_sum = local_sum + phonon_local[mode_index] * shifted
        side_sum = side_sum + phonon_side[mode_index] * shifted
    side_pad = jnp.pad(side_sum, ((0, 0), (1, 1), (0, 0), (0, 0), (0, 0)))
    return local_sum + side_pad[:, :-2] + side_pad[:, 2:]
```

```python
import functools

import jax
import jax.numpy as jnp
from jax import lax
from jax.experimental import pallas as pl
from jax.experimental.pallas import tpu as pltpu
from jax.sharding import PartitionSpec as P

MODES = 4
F32 = jnp.float32
BF16 = jnp.bfloat16
VMEM = pl.BlockSpec(memory_space=pltpu.VMEM)
SMEM = pl.BlockSpec(memory_space=pltpu.SMEM)


def split(value):
    high = value.astype(BF16)
    return high, (value - high.astype(F32)).astype(BF16)


def product(left, right):
    def dot(a, b):
        return jnp.dot(a, b, preferred_element_type=F32)

    return dot(left[0], right[0]) + (dot(left[0], right[1]) + dot(left[1], right[0]))


def parts(real, imag):
    return split(real), split(imag), split(real + imag)


def complex_product(left, right):
    first = product(left[0], right[0])
    second = product(left[1], right[1])
    third = product(left[2], right[2])
    return first - second, third - (first + second)


def start_series(real, imag):
    shape = real.shape
    eye = lax.broadcasted_iota(jnp.int32, shape, 0) == lax.broadcasted_iota(jnp.int32, shape, 1)
    diag_real = jnp.where(eye, real, 0.0)
    diag_imag = jnp.where(eye, imag, 0.0)

    def inverse(axis):
        a = jnp.sum(diag_real, axis, keepdims=True)
        b = jnp.sum(diag_imag, axis, keepdims=True)
        modulus = a * a + b * b
        return a / modulus, -b / modulus

    col_real, col_imag = inverse(0)
    row_real, row_imag = inverse(1)
    e_real = jnp.where(eye, 0.0, imag * col_imag - real * col_real)
    e_imag = jnp.where(eye, 0.0, -(real * col_imag + imag * col_real))
    t_real = e_real + jnp.where(eye, 1.0, 0.0)
    x_real = row_real * t_real - row_imag * e_imag
    x_imag = row_real * e_imag + row_imag * t_real
    return e_real, e_imag, x_real, x_imag


def is_active(step, sections):
    slot = lax.axis_index("section")
    return jnp.logical_or(slot == step, slot == sections - 1 - step)


def chain_kernel(step, sections, system, sigma, link, link_t, out):
    active = is_active(step, sections)

    @pl.when(active)
    def _():
        e_real, e_imag, x_real, x_imag = start_series(system[0] - sigma[0], system[1] - sigma[1])
        e_parts = parts(e_real, e_imag)
        square = complex_product(e_parts, e_parts)
        right = split(link[...])
        left = split(link_t[...])
        a_real = product(left, split(x_real))
        a_imag = product(left, split(x_imag))
        f_parts = parts(*square)
        b_real, b_imag = complex_product(parts(a_real, a_imag), f_parts)
        g_real, g_imag = complex_product(f_parts, f_parts)
        w_real = product(split(g_real), right) + link[...]
        w_imag = product(split(g_imag), right)
        s_real, s_imag = complex_product(
            parts(b_real + a_real, b_imag + a_imag), parts(w_real, w_imag)
        )
        out[0] = s_real
        out[1] = s_imag

    @pl.when(jnp.logical_not(active))
    def _():
        out[...] = jnp.zeros_like(out)


def green_kernel(step, sections, system, sigma, other, out_real, out_imag):
    active = is_active(step, sections)

    @pl.when(active)
    def _():
        e_real, e_imag, x_real, x_imag = start_series(
            system[0] - sigma[0] - other[0], system[1] - sigma[1] - other[1]
        )
        e_parts = parts(e_real, e_imag)
        f_parts = parts(*complex_product(e_parts, e_parts))
        b_real, b_imag = complex_product(parts(x_real, x_imag), f_parts)
        g_real, g_imag = complex_product(f_parts, f_parts)
        b_real = b_real + x_real
        b_imag = b_imag + x_imag
        s_real, s_imag = complex_product(parts(b_real, b_imag), parts(g_real, g_imag))
        out_real[...] = b_real + s_real
        out_imag[...] = b_imag + s_imag

    @pl.when(jnp.logical_not(active))
    def _():
        out_real[...] = jnp.zeros_like(out_real)
        out_imag[...] = jnp.zeros_like(out_imag)


def cost(dimension, products, arrays):
    size = dimension * dimension
    return pl.CostEstimate(
        flops=6 * products * size * dimension, bytes_accessed=4 * arrays * size, transcendentals=0
    )


def chain_step(step, sections, system, sigma, link, link_t):
    return pl.pallas_call(
        functools.partial(chain_kernel, step, sections),
        out_shape=jax.ShapeDtypeStruct(system.shape, F32),
        in_specs=[VMEM] * 4,
        out_specs=VMEM,
        cost_estimate=cost(system.shape[-1], 16, 8),
        name=f"chain{step}",
    )(system, sigma, link, link_t)


def green_step(step, sections, system, sigma, other):
    flat = jax.ShapeDtypeStruct(system.shape[1:], F32)
    return pl.pallas_call(
        functools.partial(green_kernel, step, sections),
        out_shape=(flat, flat),
        in_specs=[VMEM] * 3,
        out_specs=(VMEM, VMEM),
        cost_estimate=cost(system.shape[-1], 12, 8),
        name=f"green{step}",
    )(system, sigma, other)


def prepare_kernel(sections, scalars, onsite, hopping, coupling, born, system, links):
    flip = (lax.axis_index("section") >= sections // 2).astype(jnp.int32)
    blocks, dimension = onsite.shape
    shape = (dimension, dimension)
    eye = lax.broadcasted_iota(jnp.int32, shape, 0) == lax.broadcasted_iota(jnp.int32, shape, 1)
    energy = scalars[0]
    broad = scalars[1]
    for index in range(blocks):
        where = jnp.where(flip == 1, blocks - 1 - index, index)
        block = hopping[index]
        level = energy - onsite[pl.ds(index, 1), :]
        real = jnp.where(eye, jnp.broadcast_to(level, shape), 0.0) - 0.5 * (block + block.T)
        system[where, 0] = real - born[0, index, 0]
        system[where, 1] = jnp.where(eye, broad, 0.0) - born[0, index, 1]
    for index in range(blocks - 1):
        where = jnp.where(flip == 1, blocks - 2 - index, index)
        link = coupling[index]
        links[where, flip] = link
        links[where, 1 - flip] = link.T


def prepare(sections, scalars, onsite, hopping, coupling, born):
    blocks, dimension = onsite.shape
    return pl.pallas_call(
        functools.partial(prepare_kernel, sections),
        out_shape=(
            jax.ShapeDtypeStruct((blocks, 2, dimension, dimension), F32),
            jax.ShapeDtypeStruct((max(blocks - 1, 1), 2, dimension, dimension), F32),
        ),
        in_specs=[SMEM, VMEM, VMEM, VMEM, VMEM],
        out_specs=(VMEM, VMEM),
        name="prepare",
    )(scalars, onsite, hopping, coupling, born)


def edge_links_kernel(sections, own, before, inward, outward):
    flip = lax.axis_index("section") >= sections // 2

    @pl.when(flip)
    def _():
        inward[0] = before[...].T
        inward[1] = before[...]
        outward[0] = own[...]
        outward[1] = own[...].T

    @pl.when(jnp.logical_not(flip))
    def _():
        inward[0] = own[...]
        inward[1] = own[...].T
        outward[0] = before[...].T
        outward[1] = before[...]


def edge_links(sections, own, before):
    shape = jax.ShapeDtypeStruct((2,) + own.shape, F32)
    return pl.pallas_call(
        functools.partial(edge_links_kernel, sections),
        out_shape=(shape, shape),
        in_specs=[VMEM, VMEM],
        out_specs=(VMEM, VMEM),
        name="edge_links",
    )(own, before)


def mode_weights(shifts, weight, even):
    def at(shift):
        chosen = (shifts == shift).astype(F32)[:, None, None]
        return jnp.sum(jnp.where(chosen > 0, weight, 0.0), 0)

    low, high, far_low, far_high = at(-1), at(1), at(-2), at(2)
    return (
        at(0),
        jnp.where(even, low, high),
        jnp.where(even, high, low),
        jnp.where(even, far_low, far_high),
        jnp.where(even, far_high, far_low),
    )


def local(
    onsite, hopping, coupling, broadening, born_sigma, phonon_shift, phonon_local, phonon_side
):
    assert born_sigma.shape[0] == 1
    blocks, dimension = onsite.shape
    sections = lax.axis_size("section")
    spread = lax.axis_size("energy")
    assert sections % 2 == 0 and spread % 2 == 0
    half = sections // 2
    slot = lax.axis_index("section")
    energy_slot = lax.axis_index("energy")
    even = energy_slot % 2 == 0
    flip = slot >= half

    def over_section(value, route):
        return lax.ppermute(value, "section", route)

    def over_energy(value, step, route):
        members = sorted({step, sections - 1 - step})
        pairs = [(a * sections + s, b * sections + s) for a, b in route for s in members]
        return lax.ppermute(value, ("energy", "section"), pairs)

    swap = [(e, e ^ 1) for e in range(spread)]
    near = [(e, e + 2 if e % 2 == 0 else e - 2) for e in range(spread)]
    near = [(a, b) for a, b in near if 0 <= b < spread]
    far = [(b, a) for a, b in near]

    energy_value = -2.0 + 4.0 * energy_slot.astype(F32) / (spread - 1)
    scalars = jnp.stack([energy_value, broadening[0]])
    before = over_section(coupling[-1], [(s, s + 1) for s in range(sections - 1)])
    system, links = prepare(sections, scalars, onsite, hopping, coupling, born_sigma)
    inward, outward = edge_links(sections, coupling[-1], before)

    sigma = jnp.zeros((2, dimension, dimension), F32)
    first = [None] * blocks
    for step in range(half):
        mine = is_active(step, sections)
        for index in range(blocks):
            first[index] = sigma if step == 0 else jnp.where(mine, sigma, first[index])
            link = links[index] if index < blocks - 1 else inward
            sigma = chain_step(step, sections, system[index], sigma, link[0], link[1])
        if step < half - 1:
            route = [(step, step + 1), (sections - 1 - step, sections - 2 - step)]
        else:
            route = [(step, step + 1), (step + 1, step)]
        sigma = over_section(sigma, route)

    local_weights = lax.optimization_barrier(mode_weights(phonon_shift, phonon_local, even))
    side_weights = lax.optimization_barrier(mode_weights(phonon_shift, phonon_side, even))
    a_own, a_x, a_y, a_pair, a_lone = local_weights
    b_own, b_x, b_y, b_pair, b_lone = side_weights

    real, real_partner, imag, imag_near, imag_far = ({} for _ in range(5))
    for step in range(half, sections):
        for index in range(blocks - 1, -1, -1):
            key = (step, index)
            real[key], imag[key] = green_step(step, sections, system[index], first[index], sigma)
            real_partner[key] = over_energy(real[key], step, swap)
            imag_near[key] = over_energy(imag[key], step, near)
            imag_far[key] = over_energy(imag[key], step, far)
            if index > 0:
                sigma = chain_step(
                    step, sections, system[index], sigma, links[index - 1][1], links[index - 1][0]
                )
            elif step < sections - 1:
                sigma = chain_step(step, sections, system[index], sigma, outward[0], outward[1])
                route = [(step, step + 1), (sections - 1 - step, sections - 2 - step)]
                sigma = over_section(sigma, route)

    imag_y, imag_own = {}, {}
    for key in imag:
        imag_y[key] = b_x * imag[key] + b_y * imag_far[key]
        imag_own[key] = b_own * imag[key] + b_lone * imag_far[key] + b_pair * imag_near[key]

    def edges(table, step, index, route):
        return over_section(table[(step, index)], route)

    result = [None] * blocks
    for step in range(half, sections):
        mine = is_active(step, sections)
        outer = (sections - 1 - step, step)
        for index in range(blocks - 1, -1, -1):
            sides = []
            for table in (real, real_partner, imag_y, imag_own):
                total = None
                if index < blocks - 1:
                    total = table[(step, index + 1)]
                elif step == half:
                    total = edges(table, step, index, [outer, outer[::-1]])
                else:
                    inner = (outer[0] + 1, outer[1] - 1)
                    total = edges(
                        table, step - 1, 0, [(inner[0], outer[0]), (inner[1], outer[1])]
                    )
                if index > 0:
                    total = total + table[(step, index - 1)]
                elif step < sections - 1:
                    ends = (outer[0] - 1, outer[1] + 1)
                    total = total + edges(
                        table,
                        step + 1,
                        blocks - 1,
                        [(ends[0], outer[0]), (ends[1], outer[1])],
                    )
                sides.append(total)
            key = (step, index)
            n_real, n_partner, n_y, n_own = sides
            to_pair = (
                a_pair * real[key] + a_x * real_partner[key] + b_pair * n_real + b_x * n_partner
            )
            to_lone = a_lone * real[key] + b_lone * n_real
            to_y = a_x * imag[key] + a_y * imag_far[key] + n_y
            real_sum = a_own * real[key] + a_y * real_partner[key] + b_own * n_real + b_y * n_partner
            imag_sum = a_own * imag[key] + a_lone * imag_far[key] + a_pair * imag_near[key] + n_own
            real_sum = real_sum + over_energy(to_pair, step, near) + over_energy(to_lone, step, far)
            imag_sum = imag_sum + over_energy(to_y, step, swap)
            block = jnp.stack([real_sum, imag_sum])
            result[index] = block if step == half else jnp.where(mine, block, result[index])
    ordered = [jnp.where(flip, result[blocks - 1 - i], result[i]) for i in range(blocks)]
    return jnp.stack(ordered)[None]


def solution(mesh):
    in_specs = (
        P("section", None),
        P("section", None, None),
        P("section", None, None),
        P("energy"),
        P("energy", "section", None, None, None),
        P(),
        P(),
        P(),
    )
    out_specs = P("energy", "section", None, None, None)
    return jax.shard_map(local, mesh=mesh, in_specs=in_specs, out_specs=out_specs, check_vma=False)
```

```python
import functools

import jax
import jax.numpy as jnp
from jax import lax
from jax.experimental import pallas as pl
from jax.experimental.pallas import tpu as pltpu
from jax.sharding import PartitionSpec as P

F32 = jnp.float32
BF16 = jnp.bfloat16
VMEM = pl.BlockSpec(memory_space=pltpu.VMEM)


def split(value):
    high = value.astype(BF16)
    return high, (value - high.astype(F32)).astype(BF16)


def product(left, right):
    def dot(a, b):
        return jnp.dot(a, b, preferred_element_type=F32)

    return dot(left[0], right[0]) + (dot(left[0], right[1]) + dot(left[1], right[0]))


def parts(real, imag):
    return split(real), split(imag), split(real + imag)


def complex_product(left, right):
    first = product(left[0], right[0])
    second = product(left[1], right[1])
    third = product(left[2], right[2])
    return first - second, third - (first + second)


def start_series(real, imag):
    shape = real.shape
    eye = lax.broadcasted_iota(jnp.int32, shape, 0) == lax.broadcasted_iota(jnp.int32, shape, 1)
    diag_real = jnp.where(eye, real, 0.0)
    diag_imag = jnp.where(eye, imag, 0.0)

    def inverse(axis):
        a = jnp.sum(diag_real, axis, keepdims=True)
        b = jnp.sum(diag_imag, axis, keepdims=True)
        modulus = a * a + b * b
        return a / modulus, -b / modulus

    col_real, col_imag = inverse(0)
    row_real, row_imag = inverse(1)
    e_real = jnp.where(eye, 0.0, imag * col_imag - real * col_real)
    e_imag = jnp.where(eye, 0.0, -(real * col_imag + imag * col_real))
    t_real = e_real + jnp.where(eye, 1.0, 0.0)
    x_real = row_real * t_real - row_imag * e_imag
    x_imag = row_real * e_imag + row_imag * t_real
    return e_real, e_imag, x_real, x_imag


def is_active(step, sections):
    slot = lax.axis_index("section")
    return jnp.logical_or(slot == step, slot == sections - 1 - step)


def series_square(real, imag):
    e_real, e_imag, x_real, x_imag = start_series(real, imag)
    e_parts = parts(e_real, e_imag)
    return x_real, x_imag, parts(*complex_product(e_parts, e_parts))


def half_of(sections):
    return lax.axis_index("section") >= sections // 2


def is_at(step, sections):
    slot = lax.axis_index("section")
    return jnp.logical_or(slot == step, slot == sections - 1 - step)


def chain_core(real, imag, link, link_t, out):
    x_real, x_imag, f_parts = series_square(real, imag)
    right = split(link)
    left = split(link_t)
    a_real = product(left, split(x_real))
    a_imag = product(left, split(x_imag))
    b_real, b_imag = complex_product(parts(a_real, a_imag), f_parts)
    g_real, g_imag = complex_product(f_parts, f_parts)
    w_real = product(split(g_real), right) + link
    w_imag = product(split(g_imag), right)
    s_real, s_imag = complex_product(parts(b_real + a_real, b_imag + a_imag), parts(w_real, w_imag))
    out[0] = s_real
    out[1] = s_imag


def call(body, out_shape, operands, products, name):
    dimension = operands[0].shape[-1]
    size = dimension * dimension
    return pl.pallas_call(
        body,
        out_shape=out_shape,
        in_specs=[VMEM] * len(operands),
        out_specs=jax.tree.map(lambda _: VMEM, out_shape),
        compiler_params=pltpu.CompilerParams(vmem_limit_bytes=12 << 20),
        cost_estimate=pl.CostEstimate(
            flops=6 * products * size * dimension, bytes_accessed=4 * 8 * size, transcendentals=0
        ),
        name=name,
    )(*operands)


def link_ways(sections, refs, links):
    table, near, away = refs[0], links[0][1], links[0][2]
    if len(links) == 1:
        return table[near], table[away]
    right_half = half_of(sections)
    plain = refs[1][...]
    turned = plain.T
    link, link_t = (turned, plain) if links[1][1] else (plain, turned)
    return jnp.where(right_half, link, table[near]), jnp.where(right_half, link_t, table[away])


def chain_step(sections, active, pack, block, sigmas, links, name, after=()):
    arrays = [pack] + list(sigmas) + [link[0] for link in links]
    count = len(arrays)

    def body(*refs):
        out = refs[-1]
        source = refs[0]
        given = refs[1 : 1 + len(sigmas)]

        def work():
            real, imag = source[2 * block], source[2 * block + 1]
            if len(given) == 1:
                real, imag = real - given[0][0], imag - given[0][1]
            elif len(given) == 2:
                outer = is_at(0, sections)
                real = real - jnp.where(outer, given[0][0], given[1][0])
                imag = imag - jnp.where(outer, given[0][1], given[1][1])
            link, link_t = link_ways(sections, refs[1 + len(sigmas) : count], links)
            chain_core(real, imag, link, link_t, out)

        if active is None:
            work()
        else:
            mine = is_at(active, sections)
            pl.when(mine)(work)

            @pl.when(jnp.logical_not(mine))
            def _():
                out[...] = jnp.zeros_like(out)

    shape = jax.ShapeDtypeStruct((2,) + pack.shape[1:], F32)
    return call(body, shape, arrays + list(after), 16, name)


def green_step(sections, active, pack, block, first, second, name, passed=(), joined=()):
    arrays = [pack] + [a for a in first + second if a is not None]
    count = len(arrays)
    arrays = arrays + list(passed) + [a for pair in joined for a in pair]
    size = 1 + len(joined)

    def body(*refs):
        outs = refs[-2:]

        def put(place, value):
            if joined:
                outs[place][0] = value
            else:
                outs[place][...] = value

        def work():
            rest = list(refs[1:count])
            value = [refs[0][2 * block], refs[0][2 * block + 1]]
            outer = is_at(0, sections)
            for pair in (first, second):
                taken = [None if a is None else rest.pop(0) for a in pair]
                for place in (0, 1):
                    terms = [
                        jnp.zeros_like(value[0]) if t is None else t[place] for t in taken
                    ]
                    term = terms[0] if len(terms) == 1 else jnp.where(outer, *terms)
                    value[place] = value[place] - term
            x_real, x_imag, f_parts = series_square(*value)
            b_real, b_imag = complex_product(parts(x_real, x_imag), f_parts)
            g_real, g_imag = complex_product(f_parts, f_parts)
            b_real = b_real + x_real
            b_imag = b_imag + x_imag
            s_real, s_imag = complex_product(parts(b_real, b_imag), parts(g_real, g_imag))
            put(0, b_real + s_real)
            put(1, b_imag + s_imag)

        if active is None:
            work()
        else:
            mine = is_at(active, sections)
            pl.when(mine)(work)

            @pl.when(jnp.logical_not(mine))
            def _():
                for place in (0, 1):
                    if passed:
                        put(place, refs[count + place][...])
                    else:
                        put(place, jnp.zeros(refs[0].shape[1:], F32))

        for number in range(len(joined)):
            for place in (0, 1):
                outs[place][1 + number] = refs[count + len(passed) + 2 * number + place][...]

    flat = jax.ShapeDtypeStruct(((size,) if joined else ()) + pack.shape[1:], F32)
    return call(body, (flat, flat), arrays, 12, name)


def prepare_kernel(
    sections, spread, broadening, onsite, hopping, coupling, born, pack, edge, plain, hop, cup, sig, sems
):
    blocks, dimension = onsite.shape
    copies = []
    for index in range(blocks):
        for order, (source, target) in enumerate(
            (
                (hopping.at[index], hop.at[index]),
                (born.at[0, index], sig.at[index]),
                (coupling.at[index], cup.at[index]),
            )
        ):
            copy = pltpu.make_async_copy(source, target, sems.at[3 * index + order])
            copy.start()
            copies.append(copy)
    right_half = half_of(sections)
    flip = right_half.astype(jnp.int32)
    shape = (dimension, dimension)
    eye = lax.broadcasted_iota(jnp.int32, shape, 0) == lax.broadcasted_iota(jnp.int32, shape, 1)
    position = lax.axis_index("energy").astype(F32)
    energy = -2.0 + position * (4.0 / (spread - 1))
    broad = broadening[...]
    for index in range(blocks):
        place = jnp.where(right_half, blocks - 1 - index, index)
        copies[3 * index].wait()
        block = hop[index]
        level = energy - onsite[pl.ds(index, 1), :]
        real = jnp.where(eye, jnp.broadcast_to(level, shape), 0.0) - 0.5 * (block + block.T)
        copies[3 * index + 1].wait()
        pack[2 * place] = real - sig[index, 0]
        pack[2 * place + 1] = jnp.where(eye, jnp.broadcast_to(broad, shape), 0.0) - sig[index, 1]
        copies[3 * index + 2].wait()
        link = cup[index]
        if index < blocks - 1:
            place = 2 * blocks + 2 * jnp.where(right_half, blocks - 2 - index, index)
            pack[place + flip] = link
            pack[place + 1 - flip] = link.T
        else:
            plain[...] = link
            edge[0] = link
            edge[1] = link.T


def prepare(sections, spread, broadening, onsite, hopping, coupling, born):
    blocks, dimension = onsite.shape
    outside = pl.BlockSpec(memory_space=pltpu.HBM)
    return pl.pallas_call(
        functools.partial(prepare_kernel, sections, spread),
        out_shape=(
            jax.ShapeDtypeStruct((4 * blocks - 2, dimension, dimension), F32),
            jax.ShapeDtypeStruct((2, dimension, dimension), F32),
            jax.ShapeDtypeStruct((dimension, dimension), F32),
        ),
        in_specs=[VMEM, VMEM, outside, outside, outside],
        out_specs=(VMEM, VMEM, VMEM),
        scratch_shapes=[
            pltpu.VMEM((blocks, dimension, dimension), F32),
            pltpu.VMEM((blocks, dimension, dimension), F32),
            pltpu.VMEM((blocks, 2, dimension, dimension), F32),
            pltpu.SemaphoreType.DMA((3 * blocks,)),
        ],
        compiler_params=pltpu.CompilerParams(vmem_limit_bytes=16 << 20),
        name="prepare",
    )(broadening.reshape(1, 1), onsite, hopping, coupling, born)


OWN, NEXT, OTHER, PAIR, LONE = range(5)


def is_even():
    return lax.axis_index("energy") % 2 == 0


def first_is_far():
    slot = lax.axis_index("energy")
    return (slot // 2) % 2 == slot % 2


def weights(shifts, local_weight, side_weight, after):
    shape = jax.ShapeDtypeStruct((5,) + local_weight.shape[1:], F32)

    def body(shift_ref, local_ref, side_ref, _, local_out, side_out):
        even = is_even()
        low, high = jnp.where(even, NEXT, OTHER), jnp.where(even, OTHER, NEXT)
        far_low, far_high = jnp.where(even, PAIR, LONE), jnp.where(even, LONE, PAIR)
        for source, target in ((local_ref, local_out), (side_ref, side_out)):
            for shift, place in ((0, OWN), (-1, low), (1, high), (-2, far_low), (2, far_high)):
                total = jnp.zeros(source.shape[1:], F32)
                for mode in range(source.shape[0]):
                    total = total + jnp.where(shift_ref[mode] == shift, source[mode], 0.0)
                target[place] = total

    return pl.pallas_call(
        body,
        out_shape=(shape, shape),
        in_specs=[pl.BlockSpec(memory_space=pltpu.SMEM)] + [VMEM] * 3,
        out_specs=(VMEM, VMEM),
        compiler_params=pltpu.CompilerParams(vmem_limit_bytes=12 << 20),
        cost_estimate=pl.CostEstimate(flops=1 << 20, bytes_accessed=8 << 20, transcendentals=0),
        name="weights",
    )(shifts, local_weight, side_weight, after)


def side_terms(sections, side_weight, real, partner, imag, ahead, behind):
    blocks, dimension = real.shape[0], real.shape[-1]
    flat = (dimension, dimension)

    def body(weight, real, partner, imag, ahead, behind, for_partner, own, middle, shared):
        outer = is_at(0, sections)
        chosen = first_is_far()
        for index in range(blocks):
            far = jnp.where(chosen, ahead[index], behind[index])
            near = jnp.where(chosen, behind[index], ahead[index])
            value = imag[index]
            for_partner[index] = weight[NEXT] * value + weight[OTHER] * far
            own[index] = weight[OWN] * value + weight[LONE] * far + weight[PAIR] * near
        last = blocks - 1
        middle[0] = partner[last]
        middle[1] = for_partner[last]
        middle[2] = own[last]
        for place, table in enumerate((real, partner, for_partner, own)):
            shared[place] = jnp.where(outer, table[last], table[0])

    def shape(count):
        return jax.ShapeDtypeStruct((count,) + flat, F32)

    return call(
        body,
        (shape(blocks), shape(blocks), shape(3), shape(4)),
        [side_weight, real, partner, imag, ahead, behind],
        1,
        "side_terms",
    )


def combine(sections, tables):
    names = list(tables)
    blocks, dimension = tables["real"].shape[0], tables["real"].shape[-1]

    def body(*refs):
        t = dict(zip(names, refs))
        to_first, to_second, to_partner, own = refs[len(names) :]
        a, b = t["local_weight"], t["side_weight"]
        outer = is_at(0, sections)
        chosen = first_is_far()
        last = blocks - 1
        for index in range(blocks):
            sides = []
            for place, name in enumerate(("real", "partner", "side_partner", "side_own")):
                table = t[name]
                if index == 0:
                    side = jnp.where(outer, 0.0, t["shared"][place])
                else:
                    side = table[index - 1]
                if index < last:
                    side = side + table[index + 1]
                else:
                    middle = t["middle_real"][...] if place == 0 else t["middle"][place - 1]
                    side = side + jnp.where(outer, t["shared"][place], middle)
                sides.append(side)
            n_real, n_partner, n_for, n_own = sides
            real, partner, imag = t["real"][index], t["partner"][index], t["imag"][index]
            ahead, behind = t["ahead"][index], t["behind"][index]
            far = jnp.where(chosen, ahead, behind)
            near = jnp.where(chosen, behind, ahead)
            pair = a[PAIR] * real + a[NEXT] * partner + b[PAIR] * n_real + b[NEXT] * n_partner
            lone = a[LONE] * real + b[LONE] * n_real
            to_first[index] = jnp.where(chosen, pair, lone)
            to_second[index] = jnp.where(chosen, lone, pair)
            to_partner[index] = a[NEXT] * imag + a[OTHER] * far + n_for
            own[2 * index] = (
                a[OWN] * real + a[OTHER] * partner + b[OWN] * n_real + b[OTHER] * n_partner
            )
            own[2 * index + 1] = a[OWN] * imag + a[LONE] * far + a[PAIR] * near + n_own

    def shape(count):
        return jax.ShapeDtypeStruct((count, dimension, dimension), F32)

    return call(
        body,
        (shape(blocks), shape(blocks), shape(blocks), shape(2 * blocks)),
        [tables[name] for name in names],
        1,
        "combine",
    )


def finish(sections, own, from_first, from_second, from_partner):
    blocks, dimension = from_first.shape[0], from_first.shape[-1]

    def body(own, from_first, from_second, from_partner, out):
        right_half = half_of(sections)
        for index in range(blocks):
            place = jnp.where(right_half, blocks - 1 - index, index)
            out[0, place, 0] = own[2 * index] + (from_first[index] + from_second[index])
            out[0, place, 1] = own[2 * index + 1] + from_partner[index]

    shape = jax.ShapeDtypeStruct((1, blocks, 2, dimension, dimension), F32)
    return call(body, shape, [own, from_first, from_second, from_partner], 1, "finish")


def local(
    onsite, hopping, coupling, broadening, born_sigma, phonon_shift, phonon_local, phonon_side
):
    blocks = onsite.shape[0]
    sections = lax.axis_size("section")
    spread = lax.axis_size("energy")
    assert born_sigma.shape[0] == 1 and spread % 2 == 0
    assert sections % 4 == 0 and sections // 4 == 1 and blocks >= 2
    half = sections // 2
    last = blocks - 1
    inwards = [(0, 1), (sections - 1, sections - 2)]
    outwards = [(b, a) for a, b in inwards]
    across = [(half - 1, half), (half, half - 1)]

    def over_section(value, route):
        return lax.ppermute(value, "section", route)

    def over_energy(value, route):
        return lax.ppermute(value, "energy", route)

    swap = [(e, e ^ 1) for e in range(spread)]
    pairs = [(e, e ^ 2) for e in range(spread)]
    first_swap = [(a, b) for a, b in pairs if b < spread]
    pairs = [(e, ((e + 2) ^ 2) - 2) for e in range(spread)]
    second_swap = [(a, b) for a, b in pairs if 0 <= b < spread]

    pack, edge, plain = prepare(
        sections, spread, broadening, onsite, hopping, coupling, born_sigma
    )
    before = over_section(plain, [(s, s + 1) for s in range(half - 1, sections - 1)])

    def inner_link(table, index, reverse=False):
        place = 2 * blocks + 2 * index
        return [(table, place + 1, place) if reverse else (table, place, place + 1)]

    end_link = [(edge, 0, 1), (before, True)]
    end_back = [(edge, 1, 0), (before, False)]

    first = []
    sigma = None
    for step in range(half):
        entering = []
        for index in range(blocks):
            entering.append(sigma)
            given = [] if sigma is None else [sigma]
            link = inner_link(pack, index) if index < last else end_link
            sigma = chain_step(sections, step, pack, index, given, link, f"inward{step}{index}")
        first.append(entering)
        leaving = sigma
        sigma = over_section(sigma, inwards if step < half - 1 else across)

    local_weight, side_weight = weights(phonon_shift, phonon_local, phonon_side, leaving)
    pack_in = over_section(pack, outwards)
    arriving = sigma
    earlier = tuple(first[step][last] for step in range(half))
    sigma = over_section(arriving, outwards)
    ready = green_step(
        sections, half - 1, pack, last, earlier[1:], (arriving,), f"green{last}inner"
    )
    for index in range(last, -1, -1):
        link = inner_link(pack_in, index - 1, True) if index > 0 else end_back
        after = ready if index == last else ()
        sigma = chain_step(
            sections, 0, pack_in, index, [sigma], link, f"relay{index}", after=after
        )
    green = green_step(
        sections, 0, pack, last, earlier[:1], (sigma,), f"green{last}outer", passed=ready
    )
    second = (sigma, arriving)
    joined = []
    for index in range(last, 0, -1):
        joined.insert(0, green)
        link = inner_link(pack, index - 1, True)
        second = (
            chain_step(
                sections, None, pack, index, second, link, f"outward{index}", after=green
            ),
        )
        earlier = tuple(first[step][index - 1] for step in range(half))
        green = green_step(
            sections,
            None,
            pack,
            index - 1,
            earlier,
            second,
            f"green{index - 1}",
            joined=joined if index == 1 else (),
        )
    real, imag = green
    partner = over_energy(real, swap)
    ahead = over_energy(imag, first_swap)
    behind = over_energy(imag, second_swap)
    middle_real = over_section(joined[-1][0], across)

    side_partner, side_own, middle, shared = side_terms(
        sections, side_weight, real, partner, imag, ahead, behind
    )
    middle = over_section(middle, across)
    shared = over_section(shared, inwards + outwards)
    to_first, to_second, to_partner, own = combine(
        sections,
        {
            "local_weight": local_weight,
            "side_weight": side_weight,
            "real": real,
            "partner": partner,
            "imag": imag,
            "ahead": ahead,
            "behind": behind,
            "side_partner": side_partner,
            "side_own": side_own,
            "middle_real": middle_real,
            "middle": middle,
            "shared": shared,
        },
    )
    return finish(
        sections,
        own,
        over_energy(to_first, first_swap),
        over_energy(to_second, second_swap),
        over_energy(to_partner, swap),
    )


def solution(mesh):
    in_specs = (
        P("section", None),
        P("section", None, None),
        P("section", None, None),
        P("energy"),
        P("energy", "section", None, None, None),
        P(),
        P(),
        P(),
    )
    out_specs = P("energy", "section", None, None, None)
    return jax.shard_map(local, mesh=mesh, in_specs=in_specs, out_specs=out_specs, check_vma=False)
```

```python
import functools

import jax
import jax.numpy as jnp
from jax import lax
from jax.experimental import pallas as pl
from jax.experimental.pallas import tpu as pltpu
from jax.sharding import PartitionSpec as P


F32 = jnp.float32
BF16 = jnp.bfloat16
VMEM = pl.BlockSpec(memory_space=pltpu.VMEM)


def split(value):
    high = value.astype(BF16)
    return high, (value - high.astype(F32)).astype(BF16)


def product(left, right):
    def dot(a, b):
        return jnp.dot(a, b, preferred_element_type=F32)

    return dot(left[0], right[0]) + (dot(left[0], right[1]) + dot(left[1], right[0]))


def parts(real, imag):
    return split(real), split(imag), split(real + imag)


def complex_product(left, right):
    first = product(left[0], right[0])
    second = product(left[1], right[1])
    third = product(left[2], right[2])
    return first - second, third - (first + second)


def start_series(real, imag):
    shape = real.shape
    eye = lax.broadcasted_iota(jnp.int32, shape, 0) == lax.broadcasted_iota(jnp.int32, shape, 1)
    diag_real = jnp.where(eye, real, 0.0)
    diag_imag = jnp.where(eye, imag, 0.0)

    def inverse(axis):
        a = jnp.sum(diag_real, axis, keepdims=True)
        b = jnp.sum(diag_imag, axis, keepdims=True)
        modulus = a * a + b * b
        return a / modulus, -b / modulus

    col_real, col_imag = inverse(0)
    row_real, row_imag = inverse(1)
    e_real = jnp.where(eye, 0.0, imag * col_imag - real * col_real)
    e_imag = jnp.where(eye, 0.0, -(real * col_imag + imag * col_real))
    t_real = e_real + jnp.where(eye, 1.0, 0.0)
    x_real = row_real * t_real - row_imag * e_imag
    x_imag = row_real * e_imag + row_imag * t_real
    return e_real, e_imag, x_real, x_imag


def series_square(real, imag):
    e_real, e_imag, x_real, x_imag = start_series(real, imag)
    e_parts = parts(e_real, e_imag)
    return x_real, x_imag, parts(*complex_product(e_parts, e_parts))


def half_of(sections):
    return lax.axis_index("section") >= sections // 2


def is_at(step, sections):
    slot = lax.axis_index("section")
    return jnp.logical_or(slot == step, slot == sections - 1 - step)


def chain_core(real, imag, link, link_t, out):
    x_real, x_imag, f_parts = series_square(real, imag)
    right = split(link)
    left = split(link_t)
    a_real = product(left, split(x_real))
    a_imag = product(left, split(x_imag))
    b_real, b_imag = complex_product(parts(a_real, a_imag), f_parts)
    g_real, g_imag = complex_product(f_parts, f_parts)
    w_real = product(split(g_real), right) + link
    w_imag = product(split(g_imag), right)
    s_real, s_imag = complex_product(parts(b_real + a_real, b_imag + a_imag), parts(w_real, w_imag))
    out[0] = s_real
    out[1] = s_imag


def inverse_core(real, imag, put):
    x_real, x_imag, f_parts = series_square(real, imag)
    b_real, b_imag = complex_product(parts(x_real, x_imag), f_parts)
    g_real, g_imag = complex_product(f_parts, f_parts)
    b_real = b_real + x_real
    b_imag = b_imag + x_imag
    s_real, s_imag = complex_product(parts(b_real, b_imag), parts(g_real, g_imag))
    put(0, b_real + s_real)
    put(1, b_imag + s_imag)


def call(body, out_shape, operands, products):
    dimension = operands[0].shape[-1]
    size = dimension * dimension
    return pl.pallas_call(
        body,
        out_shape=out_shape,
        in_specs=[VMEM] * len(operands),
        out_specs=jax.tree.map(lambda _: VMEM, out_shape),
        compiler_params=pltpu.CompilerParams(vmem_limit_bytes=12 << 20),
        cost_estimate=pl.CostEstimate(
            flops=6 * products * size * dimension, bytes_accessed=4 * 8 * size, transcendentals=0
        ),
    )(*operands)


def enter_step(sections, active, coupled_half, pack, given):
    place = pack.shape[0] - 2

    def body(source, value, out):
        mine = is_at(active, sections)
        coupled = half_of(sections) if coupled_half else jnp.logical_not(half_of(sections))

        @pl.when(jnp.logical_and(mine, coupled))
        def _():
            link, link_t = split(source[place]), split(source[place + 1])
            for part in (0, 1):
                out[part] = product(split(product(link, split(value[part]))), link_t)

        @pl.when(jnp.logical_not(jnp.logical_and(mine, coupled)))
        def _():
            out[...] = value[...]

    return call(body, jax.ShapeDtypeStruct(given.shape, F32), [pack, given], 4)


def link_ways(sections, refs, links):
    ways = [(ref[link[1]], ref[link[2]]) for ref, link in zip(refs, links)]
    if len(ways) == 1:
        return ways[0]
    right_half = half_of(sections)
    return tuple(jnp.where(right_half, b, a) for a, b in zip(*ways))


def chain_step(sections, active, pack, block, sigmas, links, after=(), leaves=False):
    arrays = [pack] + list(sigmas) + [link[0] for link in links]
    count = len(arrays)

    def body(*refs):
        out = refs[-1]
        source = refs[0]
        given = refs[1 : 1 + len(sigmas)]

        def work():
            real, imag = source[2 * block], source[2 * block + 1]
            if len(given) == 1:
                real, imag = real - given[0][0], imag - given[0][1]
            elif len(given) == 2:
                outer = is_at(0, sections)
                real = real - jnp.where(outer, given[0][0], given[1][0])
                imag = imag - jnp.where(outer, given[0][1], given[1][1])
            link, link_t = link_ways(sections, refs[1 + len(sigmas) : count], links)
            if not leaves:
                chain_core(real, imag, link, link_t, out)
                return

            def put(place, value):
                out[place] = value

            right_half = half_of(sections)
            pl.when(right_half)(lambda: inverse_core(real, imag, put))
            pl.when(jnp.logical_not(right_half))(
                lambda: chain_core(real, imag, link, link_t, out)
            )

        if active is None:
            work()
        else:
            mine = is_at(active, sections)
            pl.when(mine)(work)

            @pl.when(jnp.logical_not(mine))
            def _():
                out[...] = jnp.zeros_like(out)

    shape = jax.ShapeDtypeStruct((2,) + pack.shape[1:], F32)
    return call(body, shape, arrays + list(after), 16)


def green_step(sections, active, pack, block, first, second, passed=(), joined=(), after=()):
    arrays = [pack] + [a for a in first + second if a is not None]
    count = len(arrays)
    arrays = arrays + list(passed) + [a for pair in joined for a in pair] + list(after)
    size = 1 + len(joined)

    def body(*refs):
        outs = refs[-2:]

        def put(place, value):
            if joined:
                outs[place][0] = value
            else:
                outs[place][...] = value

        def work():
            rest = list(refs[1:count])
            value = [refs[0][2 * block], refs[0][2 * block + 1]]
            outer = is_at(0, sections)
            for pair in (first, second):
                taken = [None if a is None else rest.pop(0) for a in pair]
                for place in (0, 1):
                    terms = [
                        jnp.zeros_like(value[0]) if t is None else t[place] for t in taken
                    ]
                    term = terms[0] if len(terms) == 1 else jnp.where(outer, *terms)
                    value[place] = value[place] - term
            inverse_core(*value, put)

        if active is None:
            work()
        else:
            mine = is_at(active, sections)
            pl.when(mine)(work)

            @pl.when(jnp.logical_not(mine))
            def _():
                for place in (0, 1):
                    if passed:
                        put(place, refs[count + place][...])
                    else:
                        put(place, jnp.zeros(refs[0].shape[1:], F32))

        for number in range(len(joined)):
            for place in (0, 1):
                outs[place][1 + number] = refs[count + len(passed) + 2 * number + place][...]

    flat = jax.ShapeDtypeStruct(((size,) if joined else ()) + pack.shape[1:], F32)
    return call(body, (flat, flat), arrays, 12)


def prepare_kernel(
    sections, spread, broadening, onsite, hopping, coupling, born, pack, hop, cup, sig, sems
):
    blocks, dimension = onsite.shape
    copies = []
    for index in range(blocks):
        for order, (source, target) in enumerate(
            (
                (hopping.at[index], hop.at[index]),
                (born.at[0, index], sig.at[index]),
                (coupling.at[index], cup.at[index]),
            )
        ):
            copy = pltpu.make_async_copy(source, target, sems.at[3 * index + order])
            copy.start()
            copies.append(copy)
    right_half = half_of(sections)
    flip = right_half.astype(jnp.int32)
    shape = (dimension, dimension)
    eye = lax.broadcasted_iota(jnp.int32, shape, 0) == lax.broadcasted_iota(jnp.int32, shape, 1)
    position = lax.axis_index("energy").astype(F32)
    energy = -2.0 + position * (4.0 / (spread - 1))
    broad = broadening[...]
    for index in range(blocks):
        place = jnp.where(right_half, blocks - 1 - index, index)
        copies[3 * index].wait()
        block = hop[index]
        level = energy - onsite[pl.ds(index, 1), :]
        real = jnp.where(eye, jnp.broadcast_to(level, shape), 0.0) - 0.5 * (block + block.T)
        copies[3 * index + 1].wait()
        pack[2 * place] = real - sig[index, 0]
        pack[2 * place + 1] = jnp.where(eye, jnp.broadcast_to(broad, shape), 0.0) - sig[index, 1]
        copies[3 * index + 2].wait()
        link = cup[index]
        if index < blocks - 1:
            place = 2 * blocks + 2 * jnp.where(right_half, blocks - 2 - index, index)
            pack[place + flip] = link
            pack[place + 1 - flip] = link.T
        else:
            pack[4 * blocks - 2] = link
            pack[4 * blocks - 1] = link.T


def prepare(sections, spread, broadening, onsite, hopping, coupling, born):
    blocks, dimension = onsite.shape
    outside = pl.BlockSpec(memory_space=pltpu.HBM)
    return pl.pallas_call(
        functools.partial(prepare_kernel, sections, spread),
        out_shape=jax.ShapeDtypeStruct((4 * blocks, dimension, dimension), F32),
        in_specs=[VMEM, VMEM, outside, outside, outside],
        out_specs=VMEM,
        scratch_shapes=[
            pltpu.VMEM((blocks, dimension, dimension), F32),
            pltpu.VMEM((blocks, dimension, dimension), F32),
            pltpu.VMEM((blocks, 2, dimension, dimension), F32),
            pltpu.SemaphoreType.DMA((3 * blocks,)),
        ],
        compiler_params=pltpu.CompilerParams(vmem_limit_bytes=16 << 20),
        name="prepare",
    )(broadening.reshape(1, 1), onsite, hopping, coupling, born)


OWN, NEXT, OTHER, PAIR, LONE = range(5)


def is_even():
    return lax.axis_index("energy") % 2 == 0


def first_is_far():
    slot = lax.axis_index("energy")
    return (slot // 2) % 2 == slot % 2


def weights(shifts, local_weight, side_weight, after):
    shape = jax.ShapeDtypeStruct((5,) + local_weight.shape[1:], F32)

    def body(shift_ref, local_ref, side_ref, _, local_out, side_out):
        even = is_even()
        low, high = jnp.where(even, NEXT, OTHER), jnp.where(even, OTHER, NEXT)
        far_low, far_high = jnp.where(even, PAIR, LONE), jnp.where(even, LONE, PAIR)
        for source, target in ((local_ref, local_out), (side_ref, side_out)):
            for shift, place in ((0, OWN), (-1, low), (1, high), (-2, far_low), (2, far_high)):
                total = jnp.zeros(source.shape[1:], F32)
                for mode in range(source.shape[0]):
                    total = total + jnp.where(shift_ref[mode] == shift, source[mode], 0.0)
                target[place] = total

    return pl.pallas_call(
        body,
        out_shape=(shape, shape),
        in_specs=[pl.BlockSpec(memory_space=pltpu.SMEM)] + [VMEM] * 3,
        out_specs=(VMEM, VMEM),
        compiler_params=pltpu.CompilerParams(vmem_limit_bytes=12 << 20),
        cost_estimate=pl.CostEstimate(flops=1 << 20, bytes_accessed=8 << 20, transcendentals=0),
        name="weights",
    )(shifts, local_weight, side_weight, after)


def side_terms(sections, side_weight, real, partner, imag, ahead, behind, after):
    blocks, dimension = real.shape[0], real.shape[-1]
    flat = (dimension, dimension)

    def body(weight, real, partner, imag, ahead, behind, _, for_partner, own, middle, shared):
        outer = is_at(0, sections)
        chosen = first_is_far()
        for index in range(blocks):
            far = jnp.where(chosen, ahead[index], behind[index])
            near = jnp.where(chosen, behind[index], ahead[index])
            value = imag[index]
            for_partner[index] = weight[NEXT] * value + weight[OTHER] * far
            own[index] = weight[OWN] * value + weight[LONE] * far + weight[PAIR] * near
        last = blocks - 1
        middle[0] = partner[last]
        middle[1] = for_partner[last]
        middle[2] = own[last]
        for place, table in enumerate((real, partner, for_partner, own)):
            shared[place] = jnp.where(outer, table[last], table[0])

    def shape(count):
        return jax.ShapeDtypeStruct((count,) + flat, F32)

    return call(
        body,
        (shape(blocks), shape(blocks), shape(3), shape(4)),
        [side_weight, real, partner, imag, ahead, behind, after],
        1,
    )


def combine(sections, tables):
    names = list(tables)
    blocks, dimension = tables["real"].shape[0], tables["real"].shape[-1]

    def body(*refs):
        t = dict(zip(names, refs))
        to_first, to_second, to_partner, own = refs[len(names) :]
        a, b = t["local_weight"], t["side_weight"]
        outer = is_at(0, sections)
        chosen = first_is_far()
        last = blocks - 1
        for index in range(blocks):
            sides = []
            for place, name in enumerate(("real", "partner", "side_partner", "side_own")):
                table = t[name]
                if index == 0:
                    side = jnp.where(outer, 0.0, t["shared"][place])
                else:
                    side = table[index - 1]
                if index < last:
                    side = side + table[index + 1]
                else:
                    middle = t["middle_real"][...] if place == 0 else t["middle"][place - 1]
                    side = side + jnp.where(outer, t["shared"][place], middle)
                sides.append(side)
            n_real, n_partner, n_for, n_own = sides
            real, partner, imag = t["real"][index], t["partner"][index], t["imag"][index]
            ahead, behind = t["ahead"][index], t["behind"][index]
            far = jnp.where(chosen, ahead, behind)
            near = jnp.where(chosen, behind, ahead)
            pair = a[PAIR] * real + a[NEXT] * partner + b[PAIR] * n_real + b[NEXT] * n_partner
            lone = a[LONE] * real + b[LONE] * n_real
            to_first[index] = jnp.where(chosen, pair, lone)
            to_second[index] = jnp.where(chosen, lone, pair)
            to_partner[index] = a[NEXT] * imag + a[OTHER] * far + n_for
            own[2 * index] = (
                a[OWN] * real + a[OTHER] * partner + b[OWN] * n_real + b[OTHER] * n_partner
            )
            own[2 * index + 1] = a[OWN] * imag + a[LONE] * far + a[PAIR] * near + n_own

    def shape(count):
        return jax.ShapeDtypeStruct((count, dimension, dimension), F32)

    return call(
        body,
        (shape(blocks), shape(blocks), shape(blocks), shape(2 * blocks)),
        [tables[name] for name in names],
        1,
    )


def finish(sections, own, from_first, from_second, from_partner):
    blocks, dimension = from_first.shape[0], from_first.shape[-1]

    def body(own, from_first, from_second, from_partner, out):
        right_half = half_of(sections)
        for index in range(blocks):
            place = jnp.where(right_half, blocks - 1 - index, index)
            out[0, place, 0] = own[2 * index] + (from_first[index] + from_second[index])
            out[0, place, 1] = own[2 * index + 1] + from_partner[index]

    shape = jax.ShapeDtypeStruct((1, blocks, 2, dimension, dimension), F32)
    return call(body, shape, [own, from_first, from_second, from_partner], 1)


def step(
    onsite, hopping, coupling, broadening, born_sigma, phonon_shift, phonon_local, phonon_side
):
    blocks = onsite.shape[0]
    sections = lax.axis_size("section")
    spread = lax.axis_size("energy")
    assert born_sigma.shape[0] == 1 and spread % 2 == 0
    assert sections % 4 == 0 and sections // 4 == 1 and blocks >= 2
    half = sections // 2
    last = blocks - 1
    inwards = [(0, 1), (sections - 1, sections - 2)]
    outwards = [(b, a) for a, b in inwards]
    across = [(half - 1, half), (half, half - 1)]

    def over_section(value, route):
        return lax.ppermute(value, "section", route)

    def over_energy(value, route):
        return lax.ppermute(value, "energy", route)

    swap = [(e, e ^ 1) for e in range(spread)]
    pairs = [(e, e ^ 2) for e in range(spread)]
    first_swap = [(a, b) for a, b in pairs if b < spread]
    pairs = [(e, ((e + 2) ^ 2) - 2) for e in range(spread)]
    second_swap = [(a, b) for a, b in pairs if 0 <= b < spread]

    pack = prepare(sections, spread, broadening, onsite, hopping, coupling, born_sigma)

    def inner_link(table, index, reverse=False):
        place = 2 * blocks + 2 * index
        return [(table, place + 1, place) if reverse else (table, place, place + 1)]

    end = 4 * blocks - 2

    first = []
    sigma = None
    for step in range(half):
        entering = []
        if step > 0:
            sigma = enter_step(sections, step, 1, pack, sigma)
        for index in range(blocks):
            entering.append(sigma)
            given = [] if sigma is None else [sigma]
            leaves = index == last
            link = [(pack, end, end + 1)] if leaves else inner_link(pack, index)
            sigma = chain_step(sections, step, pack, index, given, link, leaves=leaves)
        first.append(entering)
        leaving = sigma
        sigma = over_section(sigma, inwards if step < half - 1 else across)

    all_weights = weights(phonon_shift, phonon_local, phonon_side, leaving)
    local_weight, side_weight = all_weights
    pack_in = over_section(lax.optimization_barrier((pack, leaving))[0], outwards)
    arriving = enter_step(sections, half - 1, 0, pack, sigma)
    earlier = tuple(first[step][last] for step in range(half))
    sigma = over_section(arriving, outwards)
    ready = green_step(sections, half - 1, pack, last, earlier[1:], (arriving,), after=all_weights)
    for index in range(last, -1, -1):
        link = (
            inner_link(pack_in, index - 1, True)
            if index > 0
            else [(pack, end + 1, end), (pack_in, end, end + 1)]
        )
        after = ready if index == last else ()
        sigma = chain_step(sections, 0, pack_in, index, [sigma], link, after=after)
    green = green_step(sections, 0, pack, last, earlier[:1], (sigma,), passed=ready)
    second = (sigma, arriving)
    joined = []
    for index in range(last, 0, -1):
        joined.insert(0, green)
        link = inner_link(pack, index - 1, True)
        second = (
            chain_step(sections, None, pack, index, second, link, after=green),
        )
        earlier = tuple(first[step][index - 1] for step in range(half))
        green = green_step(
            sections, None, pack, index - 1, earlier, second, joined=joined if index == 1 else ()
        )
    real, imag = green
    partner = over_energy(real, swap)
    ahead = over_energy(imag, first_swap)
    behind = over_energy(imag, second_swap)
    middle_real = over_section(joined[-1][0], across)

    side_partner, side_own, middle, shared = side_terms(
        sections, side_weight, real, partner, imag, ahead, behind, middle_real
    )
    middle = over_section(middle, across)
    shared = over_section(shared, inwards + outwards)
    to_first, to_second, to_partner, own = combine(
        sections,
        {
            "local_weight": local_weight,
            "side_weight": side_weight,
            "real": real,
            "partner": partner,
            "imag": imag,
            "ahead": ahead,
            "behind": behind,
            "side_partner": side_partner,
            "side_own": side_own,
            "middle_real": middle_real,
            "middle": middle,
            "shared": shared,
        },
    )
    return finish(
        sections,
        own,
        over_energy(to_first, first_swap),
        over_energy(to_second, second_swap),
        over_energy(to_partner, swap),
    )


def solution(mesh):
    in_specs = (
        P("section", None),
        P("section", None, None),
        P("section", None, None),
        P("energy"),
        P("energy", "section", None, None, None),
        P(),
        P(),
        P(),
    )
    out_specs = P("energy", "section", None, None, None)
    return jax.shard_map(step, mesh=mesh, in_specs=in_specs, out_specs=out_specs, check_vma=False)
```

```python
import functools

import jax
import jax.numpy as jnp
from jax import lax
from jax.experimental import pallas as pl
from jax.experimental.pallas import tpu as pltpu
from jax.sharding import PartitionSpec as P


F32 = jnp.float32
BF16 = jnp.bfloat16
VMEM = pl.BlockSpec(memory_space=pltpu.VMEM)


def split(value):
    high = value.astype(BF16)
    return high, (value - high.astype(F32)).astype(BF16)


def product(left, right):
    def dot(a, b):
        return jnp.dot(a, b, preferred_element_type=F32)

    return dot(left[0], right[0]) + (dot(left[0], right[1]) + dot(left[1], right[0]))


def parts(real, imag):
    return split(real), split(imag), split(real + imag)


def complex_product(left, right):
    first = product(left[0], right[0])
    second = product(left[1], right[1])
    third = product(left[2], right[2])
    return first - second, third - (first + second)


def start_series(real, imag):
    shape = real.shape
    eye = lax.broadcasted_iota(jnp.int32, shape, 0) == lax.broadcasted_iota(jnp.int32, shape, 1)
    diag_real = jnp.where(eye, real, 0.0)
    diag_imag = jnp.where(eye, imag, 0.0)

    def inverse(axis):
        a = jnp.sum(diag_real, axis, keepdims=True)
        b = jnp.sum(diag_imag, axis, keepdims=True)
        modulus = a * a + b * b
        return a / modulus, -b / modulus

    col_real, col_imag = inverse(0)
    row_real, row_imag = inverse(1)
    e_real = jnp.where(eye, 0.0, imag * col_imag - real * col_real)
    e_imag = jnp.where(eye, 0.0, -(real * col_imag + imag * col_real))
    t_real = e_real + jnp.where(eye, 1.0, 0.0)
    x_real = row_real * t_real - row_imag * e_imag
    x_imag = row_real * e_imag + row_imag * t_real
    return e_real, e_imag, x_real, x_imag


def series_square(real, imag):
    e_real, e_imag, x_real, x_imag = start_series(real, imag)
    e_parts = parts(e_real, e_imag)
    return x_real, x_imag, parts(*complex_product(e_parts, e_parts))


def half_of(sections):
    return lax.axis_index("section") >= sections // 2


def is_at(step, sections):
    slot = lax.axis_index("section")
    return jnp.logical_or(slot == step, slot == sections - 1 - step)


def chain_core(real, imag, link, link_t, out):
    x_real, x_imag, f_parts = series_square(real, imag)
    right = split(link)
    left = split(link_t)
    a_real = product(left, split(x_real))
    a_imag = product(left, split(x_imag))
    b_real, b_imag = complex_product(parts(a_real, a_imag), f_parts)
    g_real, g_imag = complex_product(f_parts, f_parts)
    w_real = product(split(g_real), right) + link
    w_imag = product(split(g_imag), right)
    s_real, s_imag = complex_product(parts(b_real + a_real, b_imag + a_imag), parts(w_real, w_imag))
    out[0] = s_real
    out[1] = s_imag


def inverse_core(real, imag, put):
    x_real, x_imag, f_parts = series_square(real, imag)
    b_real, b_imag = complex_product(parts(x_real, x_imag), f_parts)
    g_real, g_imag = complex_product(f_parts, f_parts)
    b_real = b_real + x_real
    b_imag = b_imag + x_imag
    s_real, s_imag = complex_product(parts(b_real, b_imag), parts(g_real, g_imag))
    put(0, b_real + s_real)
    put(1, b_imag + s_imag)


def call(body, out_shape, operands, products):
    dimension = operands[0].shape[-1]
    size = dimension * dimension
    return pl.pallas_call(
        body,
        out_shape=out_shape,
        in_specs=[VMEM] * len(operands),
        out_specs=jax.tree.map(lambda _: VMEM, out_shape),
        compiler_params=pltpu.CompilerParams(vmem_limit_bytes=12 << 20),
        cost_estimate=pl.CostEstimate(
            flops=6 * products * size * dimension, bytes_accessed=4 * 8 * size, transcendentals=0
        ),
    )(*operands)


def enter_step(sections, active, coupled_half, pack, given):
    place = pack.shape[0] - 2

    def body(source, value, out):
        mine = is_at(active, sections)
        coupled = half_of(sections) if coupled_half else jnp.logical_not(half_of(sections))

        @pl.when(jnp.logical_and(mine, coupled))
        def _():
            link, link_t = split(source[place]), split(source[place + 1])
            for part in (0, 1):
                out[part] = product(split(product(link, split(value[part]))), link_t)

        @pl.when(jnp.logical_not(jnp.logical_and(mine, coupled)))
        def _():
            out[...] = value[...]

    return call(body, jax.ShapeDtypeStruct(given.shape, F32), [pack, given], 4)


def link_ways(sections, refs, links):
    ways = [(ref[link[1]], ref[link[2]]) for ref, link in zip(refs, links)]
    if len(ways) == 1:
        return ways[0]
    right_half = half_of(sections)
    return tuple(jnp.where(right_half, b, a) for a, b in zip(*ways))


def chain_step(sections, active, pack, block, sigmas, links, after=(), leaves=False):
    arrays = [pack] + list(sigmas) + [link[0] for link in links]
    count = len(arrays)

    def body(*refs):
        out = refs[-1]
        source = refs[0]
        given = refs[1 : 1 + len(sigmas)]

        def work():
            real, imag = source[2 * block], source[2 * block + 1]
            if len(given) == 1:
                real, imag = real - given[0][0], imag - given[0][1]
            elif len(given) == 2:
                outer = is_at(0, sections)
                real = real - jnp.where(outer, given[0][0], given[1][0])
                imag = imag - jnp.where(outer, given[0][1], given[1][1])
            link, link_t = link_ways(sections, refs[1 + len(sigmas) : count], links)
            if not leaves:
                chain_core(real, imag, link, link_t, out)
                return

            def put(place, value):
                out[place] = value

            right_half = half_of(sections)
            pl.when(right_half)(lambda: inverse_core(real, imag, put))
            pl.when(jnp.logical_not(right_half))(
                lambda: chain_core(real, imag, link, link_t, out)
            )

        if active is None:
            work()
        else:
            mine = is_at(active, sections)
            pl.when(mine)(work)

            @pl.when(jnp.logical_not(mine))
            def _():
                out[...] = jnp.zeros_like(out)

    shape = jax.ShapeDtypeStruct((2,) + pack.shape[1:], F32)
    return call(body, shape, arrays + list(after), 16)


def green_step(sections, active, pack, block, first, second, passed=(), joined=(), after=()):
    arrays = [pack] + [a for a in first + second if a is not None]
    count = len(arrays)
    arrays = arrays + list(passed) + [a for pair in joined for a in pair] + list(after)
    size = 1 + len(joined)

    def body(*refs):
        outs = refs[-2:]

        def put(place, value):
            if joined:
                outs[place][0] = value
            else:
                outs[place][...] = value

        def work():
            rest = list(refs[1:count])
            value = [refs[0][2 * block], refs[0][2 * block + 1]]
            outer = is_at(0, sections)
            for pair in (first, second):
                taken = [None if a is None else rest.pop(0) for a in pair]
                for place in (0, 1):
                    terms = [
                        jnp.zeros_like(value[0]) if t is None else t[place] for t in taken
                    ]
                    term = terms[0] if len(terms) == 1 else jnp.where(outer, *terms)
                    value[place] = value[place] - term
            inverse_core(*value, put)

        if active is None:
            work()
        else:
            mine = is_at(active, sections)
            pl.when(mine)(work)

            @pl.when(jnp.logical_not(mine))
            def _():
                for place in (0, 1):
                    if passed:
                        put(place, refs[count + place][...])
                    else:
                        put(place, jnp.zeros(refs[0].shape[1:], F32))

        for number in range(len(joined)):
            for place in (0, 1):
                outs[place][1 + number] = refs[count + len(passed) + 2 * number + place][...]

    flat = jax.ShapeDtypeStruct(((size,) if joined else ()) + pack.shape[1:], F32)
    return call(body, (flat, flat), arrays, 12)


def prepare_kernel(
    sections, spread, broadening, onsite, hopping, coupling, born, pack, hop, cup, sig, levels, sems
):
    blocks, dimension = onsite.shape
    copies = []
    for index in range(blocks):
        for order, (source, target) in enumerate(
            (
                (hopping.at[index], hop.at[index]),
                (born.at[0, index], sig.at[index]),
                (coupling.at[index], cup.at[index]),
            )
        ):
            copy = pltpu.make_async_copy(source, target, sems.at[3 * index + order])
            copy.start()
            copies.append(copy)
    copies.append(pltpu.make_async_copy(onsite, levels, sems.at[3 * blocks]))
    copies[-1].start()
    right_half = half_of(sections)
    flip = right_half.astype(jnp.int32)
    shape = (dimension, dimension)
    eye = lax.broadcasted_iota(jnp.int32, shape, 0) == lax.broadcasted_iota(jnp.int32, shape, 1)
    position = lax.axis_index("energy").astype(F32)
    energy = -2.0 + position * (4.0 / (spread - 1))
    copies[3 * blocks].wait()
    width = jnp.broadcast_to(broadening[...], shape)
    for index in range(blocks):
        place = jnp.where(right_half, blocks - 1 - index, index)
        copies[3 * index].wait()
        block = hop[index]
        level = energy - levels[pl.ds(index, 1), :]
        real = jnp.where(eye, jnp.broadcast_to(level, shape), 0.0) - 0.5 * (block + block.T)
        copies[3 * index + 1].wait()
        pack[2 * place] = real - sig[index, 0]
        pack[2 * place + 1] = jnp.where(eye, width, 0.0) - sig[index, 1]
        copies[3 * index + 2].wait()
        link = cup[index]
        if index < blocks - 1:
            place = 2 * blocks + 2 * jnp.where(right_half, blocks - 2 - index, index)
            pack[place + flip] = link
            pack[place + 1 - flip] = link.T
        else:
            pack[4 * blocks - 2] = link
            pack[4 * blocks - 1] = link.T


def prepare(sections, spread, broadening, onsite, hopping, coupling, born):
    blocks, dimension = onsite.shape
    outside = pl.BlockSpec(memory_space=pltpu.HBM)
    return pl.pallas_call(
        functools.partial(prepare_kernel, sections, spread),
        out_shape=jax.ShapeDtypeStruct((4 * blocks, dimension, dimension), F32),
        in_specs=[VMEM] + [outside] * 4,
        out_specs=VMEM,
        scratch_shapes=[
            pltpu.VMEM((blocks, dimension, dimension), F32),
            pltpu.VMEM((blocks, dimension, dimension), F32),
            pltpu.VMEM((blocks, 2, dimension, dimension), F32),
            pltpu.VMEM((blocks, dimension), F32),
            pltpu.SemaphoreType.DMA((3 * blocks + 1,)),
        ],
        compiler_params=pltpu.CompilerParams(vmem_limit_bytes=16 << 20),
        name="prepare",
    )(
        broadening.reshape(1, 1),
        *(
            pltpu.with_memory_space_constraint(value, pltpu.HBM)
            for value in (onsite, hopping, coupling, born)
        )
    )


OWN, NEXT, OTHER, PAIR, LONE = range(5)


def is_even():
    return lax.axis_index("energy") % 2 == 0


def first_is_far():
    slot = lax.axis_index("energy")
    return (slot // 2) % 2 == slot % 2


def weights(shifts, local_weight, side_weight, after):
    shape = jax.ShapeDtypeStruct((5,) + local_weight.shape[1:], F32)

    def body(shift_ref, local_ref, side_ref, _, local_out, side_out):
        even = is_even()
        low, high = jnp.where(even, NEXT, OTHER), jnp.where(even, OTHER, NEXT)
        far_low, far_high = jnp.where(even, PAIR, LONE), jnp.where(even, LONE, PAIR)
        for source, target in ((local_ref, local_out), (side_ref, side_out)):
            for shift, place in ((0, OWN), (-1, low), (1, high), (-2, far_low), (2, far_high)):
                total = jnp.zeros(source.shape[1:], F32)
                for mode in range(source.shape[0]):
                    total = total + jnp.where(shift_ref[mode] == shift, source[mode], 0.0)
                target[place] = total

    return pl.pallas_call(
        body,
        out_shape=(shape, shape),
        in_specs=[pl.BlockSpec(memory_space=pltpu.SMEM)] + [VMEM] * 3,
        out_specs=(VMEM, VMEM),
        compiler_params=pltpu.CompilerParams(vmem_limit_bytes=12 << 20),
        cost_estimate=pl.CostEstimate(flops=1 << 20, bytes_accessed=8 << 20, transcendentals=0),
        name="weights",
    )(shifts, local_weight, side_weight, after)


def last_blocks(*tables):
    last = tables[0].shape[0] - 1

    def body(*refs):
        for place, ref in enumerate(refs[:-1]):
            refs[-1][place] = ref[last]

    shape = jax.ShapeDtypeStruct((len(tables),) + tables[0].shape[1:], F32)
    return call(body, shape, list(tables), 1)


def side_terms(sections, side_weight, real, partner, imag, ahead, behind):
    blocks, dimension = real.shape[0], real.shape[-1]
    flat = (dimension, dimension)

    def body(weight, real, partner, imag, ahead, behind, for_partner, own, middle, shared):
        outer = is_at(0, sections)
        chosen = first_is_far()
        for index in range(blocks):
            far = jnp.where(chosen, ahead[index], behind[index])
            near = jnp.where(chosen, behind[index], ahead[index])
            value = imag[index]
            for_partner[index] = weight[NEXT] * value + weight[OTHER] * far
            own[index] = weight[OWN] * value + weight[LONE] * far + weight[PAIR] * near
        last = blocks - 1
        middle[0] = for_partner[last]
        middle[1] = own[last]
        for place, table in enumerate((real, partner, for_partner, own)):
            shared[place] = jnp.where(outer, table[last], table[0])

    def shape(count):
        return jax.ShapeDtypeStruct((count,) + flat, F32)

    return call(
        body,
        (shape(blocks), shape(blocks), shape(2), shape(4)),
        [side_weight, real, partner, imag, ahead, behind],
        1,
    )


def combine(sections, tables):
    names = list(tables)
    blocks, dimension = tables["real"].shape[0], tables["real"].shape[-1]

    def body(*refs):
        t = dict(zip(names, refs))
        to_first, to_second, to_partner, own = refs[len(names) :]
        a, b = t["local_weight"], t["side_weight"]
        outer = is_at(0, sections)
        chosen = first_is_far()
        last = blocks - 1
        for index in range(blocks):
            sides = []
            for place, name in enumerate(("real", "partner", "side_partner", "side_own")):
                table = t[name]
                if index == 0:
                    side = jnp.where(outer, 0.0, t["shared"][place])
                else:
                    side = table[index - 1]
                if index < last:
                    side = side + table[index + 1]
                else:
                    middle = t["middle_real"][place] if place < 2 else t["middle"][place - 2]
                    side = side + jnp.where(outer, t["shared"][place], middle)
                sides.append(side)
            n_real, n_partner, n_for, n_own = sides
            real, partner, imag = t["real"][index], t["partner"][index], t["imag"][index]
            ahead, behind = t["ahead"][index], t["behind"][index]
            far = jnp.where(chosen, ahead, behind)
            near = jnp.where(chosen, behind, ahead)
            pair = a[PAIR] * real + a[NEXT] * partner + b[PAIR] * n_real + b[NEXT] * n_partner
            lone = a[LONE] * real + b[LONE] * n_real
            to_first[index] = jnp.where(chosen, pair, lone)
            to_second[index] = jnp.where(chosen, lone, pair)
            to_partner[index] = a[NEXT] * imag + a[OTHER] * far + n_for
            own[2 * index] = (
                a[OWN] * real + a[OTHER] * partner + b[OWN] * n_real + b[OTHER] * n_partner
            )
            own[2 * index + 1] = a[OWN] * imag + a[LONE] * far + a[PAIR] * near + n_own

    def shape(count):
        return jax.ShapeDtypeStruct((count, dimension, dimension), F32)

    return call(
        body,
        (shape(blocks), shape(blocks), shape(blocks), shape(2 * blocks)),
        [tables[name] for name in names],
        1,
    )


def finish(sections, own, from_first, from_second, from_partner):
    blocks, dimension = from_first.shape[0], from_first.shape[-1]

    def body(own, from_first, from_second, from_partner, out):
        right_half = half_of(sections)
        for index in range(blocks):
            place = jnp.where(right_half, blocks - 1 - index, index)
            out[0, place, 0] = own[2 * index] + (from_first[index] + from_second[index])
            out[0, place, 1] = own[2 * index + 1] + from_partner[index]

    shape = jax.ShapeDtypeStruct((1, blocks, 2, dimension, dimension), F32)
    return call(body, shape, [own, from_first, from_second, from_partner], 1)


def step(
    onsite, hopping, coupling, broadening, born_sigma, phonon_shift, phonon_local, phonon_side
):
    blocks = onsite.shape[0]
    sections = lax.axis_size("section")
    spread = lax.axis_size("energy")
    assert born_sigma.shape[0] == 1 and spread % 2 == 0
    assert sections % 4 == 0 and sections // 4 == 1 and blocks >= 2
    half = sections // 2
    last = blocks - 1
    pairs = [(s, s ^ 1) for s in range(sections)]
    across = [(half - 1, half), (half, half - 1)]

    def over_section(value, route):
        return lax.ppermute(value, "section", route)

    def over_energy(value, route):
        return lax.ppermute(value, "energy", route)

    swap = [(e, e ^ 1) for e in range(spread)]
    first_swap = [(e, e ^ 2) for e in range(spread) if e ^ 2 < spread]
    second_swap = [(e, ((e + 2) ^ 2) - 2) for e in range(spread)]
    second_swap = [(a, b) for a, b in second_swap if 0 <= b < spread]
    crossing = []
    for a, b in swap:
        for s, t in across + [(0, 0), (sections - 1, sections - 1)]:
            crossing.append((a * sections + s, (b if s == t else a) * sections + t))

    pack = prepare(sections, spread, broadening, onsite, hopping, coupling, born_sigma)

    def inner_link(table, index, reverse=False):
        place = 2 * blocks + 2 * index
        return [(table, place + 1, place) if reverse else (table, place, place + 1)]

    end = 4 * blocks - 2

    first = []
    sigma = None
    for step in range(half):
        entering = []
        if step > 0:
            sigma = enter_step(sections, step, 1, pack, sigma)
        for index in range(blocks):
            entering.append(sigma)
            given = [] if sigma is None else [sigma]
            leaves = index == last
            link = [(pack, end, end + 1)] if leaves else inner_link(pack, index)
            sigma = chain_step(sections, step, pack, index, given, link, leaves=leaves)
        first.append(entering)
        leaving = sigma
        if step < half - 1:
            sigma = over_section(sigma, pairs)
        else:
            sigma = lax.ppermute(sigma, ("energy", "section"), crossing)

    all_weights = weights(phonon_shift, phonon_local, phonon_side, leaving)
    local_weight, side_weight = all_weights
    pack_in = over_section(lax.optimization_barrier((pack, leaving))[0], pairs)
    arriving = enter_step(sections, half - 1, 0, pack, sigma)
    earlier = tuple(first[step][last] for step in range(half))
    sigma = over_section(arriving, pairs)
    ready = green_step(sections, half - 1, pack, last, earlier[1:], (arriving,), after=all_weights)
    for index in range(last, -1, -1):
        link = (
            inner_link(pack_in, index - 1, True)
            if index > 0
            else [(pack, end + 1, end), (pack_in, end, end + 1)]
        )
        after = ready if index == last else ()
        sigma = chain_step(sections, 0, pack_in, index, [sigma], link, after=after)
    green = green_step(sections, 0, pack, last, earlier[:1], (sigma,), passed=ready)
    second = (sigma, arriving)
    joined = []
    for index in range(last, 0, -1):
        joined.insert(0, green)
        link = inner_link(pack, index - 1, True)
        second = (
            chain_step(sections, None, pack, index, second, link, after=green),
        )
        earlier = tuple(first[step][index - 1] for step in range(half))
        green = green_step(
            sections, None, pack, index - 1, earlier, second, joined=joined if index == 1 else ()
        )
    real, imag = green
    partner = over_energy(real, swap)
    ahead = over_energy(imag, first_swap)
    behind = over_energy(imag, second_swap)
    middle_real = over_section(last_blocks(real, partner), across)

    side_partner, side_own, middle, shared = side_terms(
        sections, side_weight, real, partner, imag, ahead, behind
    )
    middle = over_section(middle, across)
    shared = over_section(shared, pairs)
    to_first, to_second, to_partner, own = combine(
        sections,
        {
            "local_weight": local_weight,
            "side_weight": side_weight,
            "real": real,
            "partner": partner,
            "imag": imag,
            "ahead": ahead,
            "behind": behind,
            "side_partner": side_partner,
            "side_own": side_own,
            "middle_real": middle_real,
            "middle": middle,
            "shared": shared,
        },
    )
    return finish(
        sections,
        own,
        over_energy(to_first, first_swap),
        over_energy(to_second, second_swap),
        over_energy(to_partner, swap),
    )


def solution(mesh):
    in_specs = (
        P("section", None),
        P("section", None, None),
        P("section", None, None),
        P("energy"),
        P("energy", "section", None, None, None),
        P(),
        P(),
        P(),
    )
    out_specs = P("energy", "section", None, None, None)
    return jax.shard_map(step, mesh=mesh, in_specs=in_specs, out_specs=out_specs, check_vma=False)
```

```python
import functools

import jax
import jax.numpy as jnp
from jax import lax
from jax.experimental import pallas as pl
from jax.experimental.pallas import tpu as pltpu
from jax.sharding import PartitionSpec as P


F32 = jnp.float32
BF16 = jnp.bfloat16
VMEM = pl.BlockSpec(memory_space=pltpu.VMEM)


def split(value):
    high = value.astype(BF16)
    return high, (value - high.astype(F32)).astype(BF16)


def product(left, right):
    def dot(a, b):
        return jnp.dot(a, b, preferred_element_type=F32)

    return dot(left[0], right[0]) + (dot(left[0], right[1]) + dot(left[1], right[0]))


def parts(real, imag):
    return split(real), split(imag), split(real + imag)


def complex_product(left, right):
    first = product(left[0], right[0])
    second = product(left[1], right[1])
    third = product(left[2], right[2])
    return first - second, third - (first + second)


def start_series(real, imag):
    shape = real.shape
    eye = lax.broadcasted_iota(jnp.int32, shape, 0) == lax.broadcasted_iota(jnp.int32, shape, 1)
    diag_real = jnp.where(eye, real, 0.0)
    diag_imag = jnp.where(eye, imag, 0.0)

    def inverse(axis):
        a = jnp.sum(diag_real, axis, keepdims=True)
        b = jnp.sum(diag_imag, axis, keepdims=True)
        modulus = a * a + b * b
        return a / modulus, -b / modulus

    col_real, col_imag = inverse(0)
    row_real, row_imag = inverse(1)
    e_real = jnp.where(eye, 0.0, imag * col_imag - real * col_real)
    e_imag = jnp.where(eye, 0.0, -(real * col_imag + imag * col_real))
    t_real = e_real + jnp.where(eye, 1.0, 0.0)
    x_real = row_real * t_real - row_imag * e_imag
    x_imag = row_real * e_imag + row_imag * t_real
    return e_real, e_imag, x_real, x_imag


def series_square(real, imag):
    e_real, e_imag, x_real, x_imag = start_series(real, imag)
    e_parts = parts(e_real, e_imag)
    return x_real, x_imag, parts(*complex_product(e_parts, e_parts))


def half_of(sections):
    return lax.axis_index("section") >= sections // 2


def is_at(step, sections):
    slot = lax.axis_index("section")
    return jnp.logical_or(slot == step, slot == sections - 1 - step)


def chain_core(real, imag, link, link_t, out):
    x_real, x_imag, f_parts = series_square(real, imag)
    right = split(link)
    left = split(link_t)
    a_real = product(left, split(x_real))
    a_imag = product(left, split(x_imag))
    b_real, b_imag = complex_product(parts(a_real, a_imag), f_parts)
    g_real, g_imag = complex_product(f_parts, f_parts)
    w_real = product(split(g_real), right) + link
    w_imag = product(split(g_imag), right)
    s_real, s_imag = complex_product(parts(b_real + a_real, b_imag + a_imag), parts(w_real, w_imag))
    out[0] = s_real
    out[1] = s_imag


def inverse_core(real, imag, put):
    x_real, x_imag, f_parts = series_square(real, imag)
    b_real, b_imag = complex_product(parts(x_real, x_imag), f_parts)
    g_real, g_imag = complex_product(f_parts, f_parts)
    b_real = b_real + x_real
    b_imag = b_imag + x_imag
    s_real, s_imag = complex_product(parts(b_real, b_imag), parts(g_real, g_imag))
    put(0, b_real + s_real)
    put(1, b_imag + s_imag)


def call(body, out_shape, operands, products):
    dimension = operands[0].shape[-1]
    size = dimension * dimension
    return pl.pallas_call(
        body,
        out_shape=out_shape,
        in_specs=[VMEM] * len(operands),
        out_specs=jax.tree.map(lambda _: VMEM, out_shape),
        compiler_params=pltpu.CompilerParams(vmem_limit_bytes=12 << 20),
        cost_estimate=pl.CostEstimate(
            flops=6 * products * size * dimension, bytes_accessed=4 * 8 * size, transcendentals=0
        ),
    )(*operands)


def enter_step(sections, active, coupled_half, pack, given):
    place = pack.shape[0] - 2

    def body(source, value, out):
        mine = is_at(active, sections)
        coupled = half_of(sections) if coupled_half else jnp.logical_not(half_of(sections))

        @pl.when(jnp.logical_and(mine, coupled))
        def _():
            link, link_t = split(source[place]), split(source[place + 1])
            for part in (0, 1):
                out[part] = product(split(product(link, split(value[part]))), link_t)

        @pl.when(jnp.logical_not(jnp.logical_and(mine, coupled)))
        def _():
            out[...] = value[...]

    return call(body, jax.ShapeDtypeStruct(given.shape, F32), [pack, given], 4)


def link_ways(sections, refs, links):
    ways = [(ref[link[1]], ref[link[2]]) for ref, link in zip(refs, links)]
    if len(ways) == 1:
        return ways[0]
    right_half = half_of(sections)
    return tuple(jnp.where(right_half, b, a) for a, b in zip(*ways))


def chain_step(sections, active, pack, block, sigmas, links, after=(), leaves=False):
    arrays = [pack] + list(sigmas) + [link[0] for link in links]
    count = len(arrays)

    def body(*refs):
        out = refs[-1]
        source = refs[0]
        given = refs[1 : 1 + len(sigmas)]

        def work():
            real, imag = source[2 * block], source[2 * block + 1]
            if len(given) == 1:
                real, imag = real - given[0][0], imag - given[0][1]
            elif len(given) == 2:
                outer = is_at(0, sections)
                real = real - jnp.where(outer, given[0][0], given[1][0])
                imag = imag - jnp.where(outer, given[0][1], given[1][1])
            link, link_t = link_ways(sections, refs[1 + len(sigmas) : count], links)
            if not leaves:
                chain_core(real, imag, link, link_t, out)
                return

            def put(place, value):
                out[place] = value

            right_half = half_of(sections)
            pl.when(right_half)(lambda: inverse_core(real, imag, put))
            pl.when(jnp.logical_not(right_half))(
                lambda: chain_core(real, imag, link, link_t, out)
            )

        if active is None:
            work()
        else:
            mine = is_at(active, sections)
            pl.when(mine)(work)

            @pl.when(jnp.logical_not(mine))
            def _():
                out[...] = jnp.zeros_like(out)

    shape = jax.ShapeDtypeStruct((2,) + pack.shape[1:], F32)
    return call(body, shape, arrays + list(after), 16)


def green_step(sections, active, pack, block, first, second, passed=(), joined=(), after=()):
    arrays = [pack] + [a for a in first + second if a is not None]
    count = len(arrays)
    arrays = arrays + list(passed) + [a for pair in joined for a in pair] + list(after)
    size = 1 + len(joined)

    def body(*refs):
        outs = refs[-2:]

        def put(place, value):
            if joined:
                outs[place][0] = value
            else:
                outs[place][...] = value

        def work():
            rest = list(refs[1:count])
            value = [refs[0][2 * block], refs[0][2 * block + 1]]
            outer = is_at(0, sections)
            for pair in (first, second):
                taken = [None if a is None else rest.pop(0) for a in pair]
                for place in (0, 1):
                    terms = [
                        jnp.zeros_like(value[0]) if t is None else t[place] for t in taken
                    ]
                    term = terms[0] if len(terms) == 1 else jnp.where(outer, *terms)
                    value[place] = value[place] - term
            inverse_core(*value, put)

        if active is None:
            work()
        else:
            mine = is_at(active, sections)
            pl.when(mine)(work)

            @pl.when(jnp.logical_not(mine))
            def _():
                for place in (0, 1):
                    if passed:
                        put(place, refs[count + place][...])
                    else:
                        put(place, jnp.zeros(refs[0].shape[1:], F32))

        for number in range(len(joined)):
            for place in (0, 1):
                outs[place][1 + number] = refs[count + len(passed) + 2 * number + place][...]

    flat = jax.ShapeDtypeStruct(((size,) if joined else ()) + pack.shape[1:], F32)
    return call(body, (flat, flat), arrays, 12)


def prepare_kernel(
    sections, spread, broadening, onsite, hopping, coupling, born, pack, hop, cup, sig, levels, sems
):
    blocks, dimension = onsite.shape
    copies = []
    for index in range(blocks):
        for order, (source, target) in enumerate(
            (
                (hopping.at[index], hop.at[index]),
                (born.at[0, index], sig.at[index]),
                (coupling.at[index], cup.at[index]),
            )
        ):
            copy = pltpu.make_async_copy(source, target, sems.at[3 * index + order])
            copy.start()
            copies.append(copy)
    copies.append(pltpu.make_async_copy(onsite, levels, sems.at[3 * blocks]))
    copies[-1].start()
    right_half = half_of(sections)
    flip = right_half.astype(jnp.int32)
    shape = (dimension, dimension)
    eye = lax.broadcasted_iota(jnp.int32, shape, 0) == lax.broadcasted_iota(jnp.int32, shape, 1)
    position = lax.axis_index("energy").astype(F32)
    energy = -2.0 + position * (4.0 / (spread - 1))
    copies[3 * blocks].wait()
    width = jnp.broadcast_to(broadening[...], shape)
    for index in range(blocks):
        place = jnp.where(right_half, blocks - 1 - index, index)
        copies[3 * index].wait()
        block = hop[index]
        level = energy - levels[pl.ds(index, 1), :]
        real = jnp.where(eye, jnp.broadcast_to(level, shape), 0.0) - 0.5 * (block + block.T)
        copies[3 * index + 1].wait()
        pack[2 * place] = real - sig[index, 0]
        pack[2 * place + 1] = jnp.where(eye, width, 0.0) - sig[index, 1]
        copies[3 * index + 2].wait()
        link = cup[index]
        if index < blocks - 1:
            place = 2 * blocks + 2 * jnp.where(right_half, blocks - 2 - index, index)
            pack[place + flip] = link
            pack[place + 1 - flip] = link.T
        else:
            pack[4 * blocks - 2] = link
            pack[4 * blocks - 1] = link.T


def prepare(sections, spread, broadening, onsite, hopping, coupling, born):
    blocks, dimension = onsite.shape
    outside = pl.BlockSpec(memory_space=pltpu.HBM)
    return pl.pallas_call(
        functools.partial(prepare_kernel, sections, spread),
        out_shape=jax.ShapeDtypeStruct((4 * blocks, dimension, dimension), F32),
        in_specs=[VMEM] + [outside] * 4,
        out_specs=VMEM,
        scratch_shapes=[
            pltpu.VMEM((blocks, dimension, dimension), F32),
            pltpu.VMEM((blocks, dimension, dimension), F32),
            pltpu.VMEM((blocks, 2, dimension, dimension), F32),
            pltpu.VMEM((blocks, dimension), F32),
            pltpu.SemaphoreType.DMA((3 * blocks + 1,)),
        ],
        compiler_params=pltpu.CompilerParams(vmem_limit_bytes=16 << 20),
        name="prepare",
    )(
        broadening.reshape(1, 1),
        *(
            pltpu.with_memory_space_constraint(value, pltpu.HBM)
            for value in (onsite, hopping, coupling, born)
        )
    )


OWN, NEXT, OTHER, PAIR, LONE = range(5)


def is_even():
    return lax.axis_index("energy") % 2 == 0


def first_is_far():
    slot = lax.axis_index("energy")
    return (slot // 2) % 2 == slot % 2


def weights(shifts, local_weight, side_weight, after):
    shape = jax.ShapeDtypeStruct((5,) + local_weight.shape[1:], F32)

    def body(shift_ref, local_ref, side_ref, _, local_out, side_out):
        even = is_even()
        low, high = jnp.where(even, NEXT, OTHER), jnp.where(even, OTHER, NEXT)
        far_low, far_high = jnp.where(even, PAIR, LONE), jnp.where(even, LONE, PAIR)
        for source, target in ((local_ref, local_out), (side_ref, side_out)):
            for shift, place in ((0, OWN), (-1, low), (1, high), (-2, far_low), (2, far_high)):
                total = jnp.zeros(source.shape[1:], F32)
                for mode in range(source.shape[0]):
                    total = total + jnp.where(shift_ref[mode] == shift, source[mode], 0.0)
                target[place] = total

    return pl.pallas_call(
        body,
        out_shape=(shape, shape),
        in_specs=[pl.BlockSpec(memory_space=pltpu.SMEM)] + [VMEM] * 3,
        out_specs=(VMEM, VMEM),
        compiler_params=pltpu.CompilerParams(vmem_limit_bytes=12 << 20),
        cost_estimate=pl.CostEstimate(flops=1 << 20, bytes_accessed=8 << 20, transcendentals=0),
        name="weights",
    )(shifts, local_weight, side_weight, after)


def last_blocks(*tables):
    last = tables[0].shape[0] - 1

    def body(*refs):
        for place, ref in enumerate(refs[:-1]):
            refs[-1][place] = ref[last]

    shape = jax.ShapeDtypeStruct((len(tables),) + tables[0].shape[1:], F32)
    return call(body, shape, list(tables), 1)


def side_terms(sections, side_weight, real, partner, imag, ahead, behind):
    blocks, dimension = real.shape[0], real.shape[-1]
    flat = (dimension, dimension)

    def body(weight, real, partner, imag, ahead, behind, for_partner, own, middle, shared):
        outer = is_at(0, sections)
        chosen = first_is_far()
        for index in range(blocks):
            far = jnp.where(chosen, ahead[index], behind[index])
            near = jnp.where(chosen, behind[index], ahead[index])
            value = imag[index]
            for_partner[index] = weight[NEXT] * value + weight[OTHER] * far
            own[index] = weight[OWN] * value + weight[LONE] * far + weight[PAIR] * near
        last = blocks - 1
        middle[0] = for_partner[last]
        middle[1] = own[last]
        for place, table in enumerate((real, partner, for_partner, own)):
            shared[place] = jnp.where(outer, table[last], table[0])

    def shape(count):
        return jax.ShapeDtypeStruct((count,) + flat, F32)

    return call(
        body,
        (shape(blocks), shape(blocks), shape(2), shape(4)),
        [side_weight, real, partner, imag, ahead, behind],
        1,
    )


def combine(sections, tables, early):
    names = list(tables)
    blocks, dimension = tables["real"].shape[0], tables["real"].shape[-1]
    last = blocks - 1
    count = 1 if early else last

    def body(*refs):
        t = dict(zip(names, refs))
        to_first, to_second, to_partner, own = refs[len(names) :]
        a, b = t["local_weight"], t["side_weight"]
        chosen = first_is_far()

        def emit(place, index, ends):
            sides = []
            for number, name in enumerate(("real", "partner", "side_partner", "side_own")):
                terms = [t[name][i] for i in (index - 1, index + 1) if 0 <= i <= last]
                terms += [end(number) for end in ends]
                sides.append(functools.reduce(jnp.add, terms))
            n_real, n_partner, n_for, n_own = sides
            real, partner, imag = t["real"][index], t["partner"][index], t["imag"][index]
            ahead, behind = t["ahead"][index], t["behind"][index]
            far = jnp.where(chosen, ahead, behind)
            near = jnp.where(chosen, behind, ahead)
            pair = a[PAIR] * real + a[NEXT] * partner + b[PAIR] * n_real + b[NEXT] * n_partner
            lone = a[LONE] * real + b[LONE] * n_real
            to_first[place] = jnp.where(chosen, pair, lone)
            to_second[place] = jnp.where(chosen, lone, pair)
            to_partner[place] = a[NEXT] * imag + a[OTHER] * far + n_for
            own[2 * place] = (
                a[OWN] * real + a[OTHER] * partner + b[OWN] * n_real + b[OTHER] * n_partner
            )
            own[2 * place + 1] = a[OWN] * imag + a[LONE] * far + a[PAIR] * near + n_own

        def middle(number):
            return t["middle_real"][number] if number < 2 else t["middle"][number - 2]

        def shared(number):
            return t["shared"][number]

        outer = is_at(0, sections)

        @pl.when(outer)
        def _():
            for place in range(count):
                index = 0 if early else place + 1
                emit(place, index, [shared] if not early and index == last else [])

        @pl.when(jnp.logical_not(outer))
        def _():
            for place in range(count):
                index = last if early else place
                emit(place, index, [middle] if early else [shared] if index == 0 else [])

    def shape(count):
        return jax.ShapeDtypeStruct((count, dimension, dimension), F32)

    return call(
        body,
        (shape(count), shape(count), shape(count), shape(2 * count)),
        [tables[name] for name in names],
        1,
    )


def finish(sections, early, late):
    blocks, dimension = 1 + late[1].shape[0], late[1].shape[-1]
    last = blocks - 1

    def body(*refs):
        out = refs[-1]
        right_half = half_of(sections)
        outer = is_at(0, sections)
        for number, group in enumerate((refs[:4], refs[4:8])):
            own, from_first, from_second, from_partner = group
            for k in range(1 if number == 0 else last):
                low, high = (0, last) if number == 0 else (k + 1, k)
                index = jnp.where(outer, low, high)
                place = jnp.where(right_half, last - index, index)
                out[0, place, 0] = own[2 * k] + (from_first[k] + from_second[k])
                out[0, place, 1] = own[2 * k + 1] + from_partner[k]

    shape = jax.ShapeDtypeStruct((1, blocks, 2, dimension, dimension), F32)
    return call(body, shape, list(early) + list(late), 1)


def step(
    onsite, hopping, coupling, broadening, born_sigma, phonon_shift, phonon_local, phonon_side
):
    blocks = onsite.shape[0]
    sections = lax.axis_size("section")
    spread = lax.axis_size("energy")
    assert born_sigma.shape[0] == 1 and spread % 2 == 0
    assert sections % 4 == 0 and sections // 4 == 1 and blocks >= 2
    half = sections // 2
    last = blocks - 1
    pairs = [(s, s ^ 1) for s in range(sections)]
    across = [(half - 1, half), (half, half - 1)]

    def over_section(value, route):
        return lax.ppermute(value, "section", route)

    def over_energy(value, route):
        return lax.ppermute(value, "energy", route)

    swap = [(e, e ^ 1) for e in range(spread)]
    first_swap = [(e, e ^ 2) for e in range(spread) if e ^ 2 < spread]
    second_swap = [(e, ((e + 2) ^ 2) - 2) for e in range(spread)]
    second_swap = [(a, b) for a, b in second_swap if 0 <= b < spread]
    crossing = []
    for a, b in swap:
        for s, t in across + [(0, 0), (sections - 1, sections - 1)]:
            crossing.append((a * sections + s, (b if s == t else a) * sections + t))

    pack = prepare(sections, spread, broadening, onsite, hopping, coupling, born_sigma)

    def inner_link(table, index, reverse=False):
        place = 2 * blocks + 2 * index
        return [(table, place + 1, place) if reverse else (table, place, place + 1)]

    end = 4 * blocks - 2

    first = []
    sigma = None
    for step in range(half):
        entering = []
        if step > 0:
            sigma = enter_step(sections, step, 1, pack, sigma)
        for index in range(blocks):
            entering.append(sigma)
            given = [] if sigma is None else [sigma]
            leaves = index == last
            link = [(pack, end, end + 1)] if leaves else inner_link(pack, index)
            sigma = chain_step(sections, step, pack, index, given, link, leaves=leaves)
        first.append(entering)
        leaving = sigma
        if step < half - 1:
            sigma = over_section(sigma, pairs)
        else:
            sigma = lax.ppermute(sigma, ("energy", "section"), crossing)

    all_weights = weights(phonon_shift, phonon_local, phonon_side, leaving)
    local_weight, side_weight = all_weights
    pack_in = over_section(pack, pairs)
    arriving = enter_step(sections, half - 1, 0, pack, sigma)
    earlier = tuple(first[step][last] for step in range(half))
    sigma = over_section(arriving, pairs)
    ready = green_step(sections, half - 1, pack, last, earlier[1:], (arriving,), after=all_weights)
    for index in range(last, -1, -1):
        link = (
            inner_link(pack_in, index - 1, True)
            if index > 0
            else [(pack, end + 1, end), (pack_in, end, end + 1)]
        )
        after = ready if index == last else ()
        sigma = chain_step(sections, 0, pack_in, index, [sigma], link, after=after)
    green = green_step(sections, 0, pack, last, earlier[:1], (sigma,), passed=ready)
    second = (sigma, arriving)
    joined = []
    for index in range(last, 0, -1):
        joined.insert(0, green)
        link = inner_link(pack, index - 1, True)
        second = (
            chain_step(sections, None, pack, index, second, link, after=green),
        )
        earlier = tuple(first[step][index - 1] for step in range(half))
        green = green_step(
            sections, None, pack, index - 1, earlier, second, joined=joined if index == 1 else ()
        )
    real, imag = green
    partner = over_energy(real, swap)
    ahead = over_energy(imag, first_swap)
    behind = over_energy(imag, second_swap)
    middle_real = over_section(last_blocks(real, partner), across)

    side_partner, side_own, middle, shared = side_terms(
        sections, side_weight, real, partner, imag, ahead, behind
    )
    middle = over_section(middle, across)
    shared = over_section(shared, pairs)
    tables = {
        "local_weight": local_weight,
        "side_weight": side_weight,
        "real": real,
        "partner": partner,
        "imag": imag,
        "ahead": ahead,
        "behind": behind,
        "side_partner": side_partner,
        "side_own": side_own,
    }

    def exchange(to_first, to_second, to_partner, own):
        from_first = over_energy(to_first, first_swap)
        from_second = over_energy(to_second, second_swap)
        from_partner = over_energy(to_partner, swap)
        return own, from_first, from_second, from_partner

    ends = {"middle_real": middle_real, "middle": middle}
    early = combine(sections, tables | ends, True)
    early = exchange(*early)
    late = combine(sections, tables | {"shared": shared}, False)
    late = exchange(*late)
    return finish(sections, early, late)


def solution(mesh):
    in_specs = (
        P("section", None),
        P("section", None, None),
        P("section", None, None),
        P("energy"),
        P("energy", "section", None, None, None),
        P(),
        P(),
        P(),
    )
    out_specs = P("energy", "section", None, None, None)
    return jax.shard_map(step, mesh=mesh, in_specs=in_specs, out_specs=out_specs, check_vma=False)
```

```python
import functools

import jax
import jax.numpy as jnp
from jax import lax
from jax.experimental import pallas as pl
from jax.experimental.pallas import tpu as pltpu
from jax.sharding import PartitionSpec as P


F32 = jnp.float32
BF16 = jnp.bfloat16
VMEM = pl.BlockSpec(memory_space=pltpu.VMEM)


def split(value):
    high = value.astype(BF16)
    return high, (value - high.astype(F32)).astype(BF16)


def product(left, right):
    def dot(a, b):
        return jnp.dot(a, b, preferred_element_type=F32)

    return dot(left[0], right[0]) + (dot(left[0], right[1]) + dot(left[1], right[0]))


def parts(real, imag):
    return split(real), split(imag), split(real + imag)


def complex_product(left, right):
    first = product(left[0], right[0])
    second = product(left[1], right[1])
    third = product(left[2], right[2])
    return first - second, third - (first + second)


def start_series(real, imag):
    shape = real.shape
    eye = lax.broadcasted_iota(jnp.int32, shape, 0) == lax.broadcasted_iota(jnp.int32, shape, 1)
    diag_real = jnp.where(eye, real, 0.0)
    diag_imag = jnp.where(eye, imag, 0.0)

    def inverse(axis):
        a = jnp.sum(diag_real, axis, keepdims=True)
        b = jnp.sum(diag_imag, axis, keepdims=True)
        modulus = a * a + b * b
        return a / modulus, -b / modulus

    col_real, col_imag = inverse(0)
    row_real, row_imag = inverse(1)
    e_real = jnp.where(eye, 0.0, imag * col_imag - real * col_real)
    e_imag = jnp.where(eye, 0.0, -(real * col_imag + imag * col_real))
    t_real = e_real + jnp.where(eye, 1.0, 0.0)
    x_real = row_real * t_real - row_imag * e_imag
    x_imag = row_real * e_imag + row_imag * t_real
    return e_real, e_imag, x_real, x_imag


def series_square(real, imag):
    e_real, e_imag, x_real, x_imag = start_series(real, imag)
    e_parts = parts(e_real, e_imag)
    return x_real, x_imag, parts(*complex_product(e_parts, e_parts))


def half_of(sections):
    return lax.axis_index("section") >= sections // 2


def is_at(step, sections):
    slot = lax.axis_index("section")
    return jnp.logical_or(slot == step, slot == sections - 1 - step)


def chain_core(real, imag, link, link_t, out):
    x_real, x_imag, f_parts = series_square(real, imag)
    right = split(link)
    left = split(link_t)
    a_real = product(left, split(x_real))
    a_imag = product(left, split(x_imag))
    b_real, b_imag = complex_product(parts(a_real, a_imag), f_parts)
    g_real, g_imag = complex_product(f_parts, f_parts)
    w_real = product(split(g_real), right) + link
    w_imag = product(split(g_imag), right)
    s_real, s_imag = complex_product(parts(b_real + a_real, b_imag + a_imag), parts(w_real, w_imag))
    out[0] = s_real
    out[1] = s_imag


def inverse_core(real, imag, put):
    x_real, x_imag, f_parts = series_square(real, imag)
    b_real, b_imag = complex_product(parts(x_real, x_imag), f_parts)
    g_real, g_imag = complex_product(f_parts, f_parts)
    b_real = b_real + x_real
    b_imag = b_imag + x_imag
    s_real, s_imag = complex_product(parts(b_real, b_imag), parts(g_real, g_imag))
    put(0, b_real + s_real)
    put(1, b_imag + s_imag)


def call(body, out_shape, operands, products):
    dimension = operands[0].shape[-1]
    size = dimension * dimension
    return pl.pallas_call(
        body,
        out_shape=out_shape,
        in_specs=[VMEM] * len(operands),
        out_specs=jax.tree.map(lambda _: VMEM, out_shape),
        compiler_params=pltpu.CompilerParams(vmem_limit_bytes=12 << 20),
        cost_estimate=pl.CostEstimate(
            flops=6 * products * size * dimension, bytes_accessed=4 * 8 * size, transcendentals=0
        ),
    )(*operands)


def enter_step(sections, active, coupled_half, pack, given):
    place = pack.shape[0] - 2

    def body(source, value, out):
        mine = is_at(active, sections)
        coupled = half_of(sections) if coupled_half else jnp.logical_not(half_of(sections))

        @pl.when(jnp.logical_and(mine, coupled))
        def _():
            link, link_t = split(source[place]), split(source[place + 1])
            for part in (0, 1):
                out[part] = product(split(product(link, split(value[part]))), link_t)

        @pl.when(jnp.logical_not(jnp.logical_and(mine, coupled)))
        def _():
            out[...] = value[...]

    return call(body, jax.ShapeDtypeStruct(given.shape, F32), [pack, given], 4)


def link_ways(sections, refs, links):
    ways = [(ref[link[1]], ref[link[2]]) for ref, link in zip(refs, links)]
    if len(ways) == 1:
        return ways[0]
    right_half = half_of(sections)
    return tuple(jnp.where(right_half, b, a) for a, b in zip(*ways))


def chain_step(sections, active, pack, block, sigmas, links, after=(), leaves=False):
    arrays = [pack] + list(sigmas) + [link[0] for link in links]
    count = len(arrays)

    def body(*refs):
        out = refs[-1]
        source = refs[0]
        given = refs[1 : 1 + len(sigmas)]

        def work():
            real, imag = source[2 * block], source[2 * block + 1]
            if len(given) == 1:
                real, imag = real - given[0][0], imag - given[0][1]
            elif len(given) == 2:
                outer = is_at(0, sections)
                real = real - jnp.where(outer, given[0][0], given[1][0])
                imag = imag - jnp.where(outer, given[0][1], given[1][1])
            link, link_t = link_ways(sections, refs[1 + len(sigmas) : count], links)
            if not leaves:
                chain_core(real, imag, link, link_t, out)
                return

            def put(place, value):
                out[place] = value

            right_half = half_of(sections)
            pl.when(right_half)(lambda: inverse_core(real, imag, put))
            pl.when(jnp.logical_not(right_half))(
                lambda: chain_core(real, imag, link, link_t, out)
            )

        if active is None:
            work()
        else:
            mine = is_at(active, sections)
            pl.when(mine)(work)

            @pl.when(jnp.logical_not(mine))
            def _():
                out[...] = jnp.zeros_like(out)

    shape = jax.ShapeDtypeStruct((2,) + pack.shape[1:], F32)
    return call(body, shape, arrays + list(after), 16)


def green_step(sections, active, pack, block, first, second, passed=(), joined=(), after=()):
    arrays = [pack] + [a for a in first + second if a is not None]
    count = len(arrays)
    arrays = arrays + list(passed) + [a for pair in joined for a in pair] + list(after)
    size = 1 + len(joined)

    def body(*refs):
        outs = refs[-2:]

        def put(place, value):
            if joined:
                outs[place][0] = value
            else:
                outs[place][...] = value

        def work():
            rest = list(refs[1:count])
            value = [refs[0][2 * block], refs[0][2 * block + 1]]
            outer = is_at(0, sections)
            for pair in (first, second):
                taken = [None if a is None else rest.pop(0) for a in pair]
                for place in (0, 1):
                    terms = [
                        jnp.zeros_like(value[0]) if t is None else t[place] for t in taken
                    ]
                    term = terms[0] if len(terms) == 1 else jnp.where(outer, *terms)
                    value[place] = value[place] - term
            inverse_core(*value, put)

        if active is None:
            work()
        else:
            mine = is_at(active, sections)
            pl.when(mine)(work)

            @pl.when(jnp.logical_not(mine))
            def _():
                for place in (0, 1):
                    if passed:
                        put(place, refs[count + place][...])
                    else:
                        put(place, jnp.zeros(refs[0].shape[1:], F32))

        for number in range(len(joined)):
            for place in (0, 1):
                outs[place][1 + number] = refs[count + len(passed) + 2 * number + place][...]

    flat = jax.ShapeDtypeStruct(((size,) if joined else ()) + pack.shape[1:], F32)
    return call(body, (flat, flat), arrays, 12)


def prepare_kernel(
    sections, spread, broadening, onsite, hopping, coupling, born, pack, hop, cup, sig, levels, sems
):
    blocks, dimension = onsite.shape
    copies = []
    for index in range(blocks):
        for order, (source, target) in enumerate(
            (
                (hopping.at[index], hop.at[index]),
                (born.at[0, index], sig.at[index]),
                (coupling.at[index], cup.at[index]),
            )
        ):
            copy = pltpu.make_async_copy(source, target, sems.at[3 * index + order])
            copy.start()
            copies.append(copy)
    copies.append(pltpu.make_async_copy(onsite, levels, sems.at[3 * blocks]))
    copies[-1].start()
    right_half = half_of(sections)
    flip = right_half.astype(jnp.int32)
    shape = (dimension, dimension)
    eye = lax.broadcasted_iota(jnp.int32, shape, 0) == lax.broadcasted_iota(jnp.int32, shape, 1)
    position = lax.axis_index("energy").astype(F32)
    energy = -2.0 + position * (4.0 / (spread - 1))
    copies[3 * blocks].wait()
    width = jnp.broadcast_to(broadening[...], shape)
    for index in range(blocks):
        place = jnp.where(right_half, blocks - 1 - index, index)
        copies[3 * index].wait()
        block = hop[index]
        level = energy - levels[pl.ds(index, 1), :]
        real = jnp.where(eye, jnp.broadcast_to(level, shape), 0.0) - 0.5 * (block + block.T)
        copies[3 * index + 1].wait()
        pack[2 * place] = real - sig[index, 0]
        pack[2 * place + 1] = jnp.where(eye, width, 0.0) - sig[index, 1]
        copies[3 * index + 2].wait()
        link = cup[index]
        if index < blocks - 1:
            place = 2 * blocks + 2 * jnp.where(right_half, blocks - 2 - index, index)
            pack[place + flip] = link
            pack[place + 1 - flip] = link.T
        else:
            pack[4 * blocks - 2] = link
            pack[4 * blocks - 1] = link.T


def prepare(sections, spread, broadening, onsite, hopping, coupling, born):
    blocks, dimension = onsite.shape
    outside = pl.BlockSpec(memory_space=pltpu.HBM)
    return pl.pallas_call(
        functools.partial(prepare_kernel, sections, spread),
        out_shape=jax.ShapeDtypeStruct((4 * blocks, dimension, dimension), F32),
        in_specs=[VMEM] + [outside] * 4,
        out_specs=VMEM,
        scratch_shapes=[
            pltpu.VMEM((blocks, dimension, dimension), F32),
            pltpu.VMEM((blocks, dimension, dimension), F32),
            pltpu.VMEM((blocks, 2, dimension, dimension), F32),
            pltpu.VMEM((blocks, dimension), F32),
            pltpu.SemaphoreType.DMA((3 * blocks + 1,)),
        ],
        compiler_params=pltpu.CompilerParams(vmem_limit_bytes=16 << 20),
        name="prepare",
    )(
        broadening.reshape(1, 1),
        *(
            pltpu.with_memory_space_constraint(value, pltpu.HBM)
            for value in (onsite, hopping, coupling, born)
        )
    )


OWN, NEXT, OTHER, PAIR, LONE = range(5)


def is_even():
    return lax.axis_index("energy") % 2 == 0


def first_is_far():
    slot = lax.axis_index("energy")
    return (slot // 2) % 2 == slot % 2


def weights(shifts, local_weight, side_weight, after):
    shape = jax.ShapeDtypeStruct((5,) + local_weight.shape[1:], F32)

    def body(shift_ref, local_ref, side_ref, _, local_out, side_out):
        even = is_even()
        low, high = jnp.where(even, NEXT, OTHER), jnp.where(even, OTHER, NEXT)
        far_low, far_high = jnp.where(even, PAIR, LONE), jnp.where(even, LONE, PAIR)
        for source, target in ((local_ref, local_out), (side_ref, side_out)):
            for shift, place in ((0, OWN), (-1, low), (1, high), (-2, far_low), (2, far_high)):
                total = jnp.zeros(source.shape[1:], F32)
                for mode in range(source.shape[0]):
                    total = total + jnp.where(shift_ref[mode] == shift, source[mode], 0.0)
                target[place] = total

    return pl.pallas_call(
        body,
        out_shape=(shape, shape),
        in_specs=[pl.BlockSpec(memory_space=pltpu.SMEM)] + [VMEM] * 3,
        out_specs=(VMEM, VMEM),
        compiler_params=pltpu.CompilerParams(vmem_limit_bytes=12 << 20),
        cost_estimate=pl.CostEstimate(flops=1 << 20, bytes_accessed=8 << 20, transcendentals=0),
        name="weights",
    )(shifts, local_weight, side_weight, after)


def last_blocks(*tables):
    last = tables[0].shape[0] - 1

    def body(*refs):
        for place, ref in enumerate(refs[:-1]):
            refs[-1][place] = ref[last]

    shape = jax.ShapeDtypeStruct((len(tables),) + tables[0].shape[1:], F32)
    return call(body, shape, list(tables), 1)


def side_terms(sections, side_weight, real, partner, imag, ahead, behind):
    blocks, dimension = real.shape[0], real.shape[-1]
    flat = (dimension, dimension)

    def body(weight, real, partner, imag, ahead, behind, for_partner, own, middle, shared):
        outer = is_at(0, sections)
        chosen = first_is_far()
        for index in range(blocks):
            far = jnp.where(chosen, ahead[index], behind[index])
            near = jnp.where(chosen, behind[index], ahead[index])
            value = imag[index]
            for_partner[index] = weight[NEXT] * value + weight[OTHER] * far
            own[index] = weight[OWN] * value + weight[LONE] * far + weight[PAIR] * near
        last = blocks - 1
        middle[0] = for_partner[last]
        middle[1] = own[last]
        for place, table in enumerate((real, partner, for_partner, own)):
            shared[place] = jnp.where(outer, table[last], table[0])

    def shape(count):
        return jax.ShapeDtypeStruct((count,) + flat, F32)

    return call(
        body,
        (shape(blocks), shape(blocks), shape(2), shape(4)),
        [side_weight, real, partner, imag, ahead, behind],
        1,
    )


def combine(sections, tables, early):
    names = list(tables)
    blocks, dimension = tables["real"].shape[0], tables["real"].shape[-1]
    last = blocks - 1
    count = 1 if early else last

    def body(*refs):
        t = dict(zip(names, refs))
        to_first, to_second, to_partner, own = refs[len(names) :]
        a, b = t["local_weight"], t["side_weight"]
        chosen = first_is_far()

        def emit(place, index, ends):
            sides = []
            for number, name in enumerate(("real", "partner", "side_partner", "side_own")):
                terms = [t[name][i] for i in (index - 1, index + 1) if 0 <= i <= last]
                terms += [end(number) for end in ends]
                sides.append(functools.reduce(jnp.add, terms))
            n_real, n_partner, n_for, n_own = sides
            real, partner, imag = t["real"][index], t["partner"][index], t["imag"][index]
            ahead, behind = t["ahead"][index], t["behind"][index]
            far = jnp.where(chosen, ahead, behind)
            near = jnp.where(chosen, behind, ahead)
            pair = a[PAIR] * real + a[NEXT] * partner + b[PAIR] * n_real + b[NEXT] * n_partner
            lone = a[LONE] * real + b[LONE] * n_real
            to_first[place] = jnp.where(chosen, pair, lone)
            to_second[place] = jnp.where(chosen, lone, pair)
            to_partner[place] = a[NEXT] * imag + a[OTHER] * far + n_for
            own[2 * place] = (
                a[OWN] * real + a[OTHER] * partner + b[OWN] * n_real + b[OTHER] * n_partner
            )
            own[2 * place + 1] = a[OWN] * imag + a[LONE] * far + a[PAIR] * near + n_own

        def middle(number):
            return t["middle_real"][number] if number < 2 else t["middle"][number - 2]

        def shared(number):
            return t["shared"][number]

        outer = is_at(0, sections)

        @pl.when(outer)
        def _():
            for place in range(count):
                index = 0 if early else place + 1
                emit(place, index, [shared] if not early and index == last else [])

        @pl.when(jnp.logical_not(outer))
        def _():
            for place in range(count):
                index = last if early else place
                emit(place, index, [middle] if early else [shared] if index == 0 else [])

    def shape(count):
        return jax.ShapeDtypeStruct((count, dimension, dimension), F32)

    return call(
        body,
        (shape(count), shape(count), shape(count), shape(2 * count)),
        [tables[name] for name in names],
        1,
    )


def finish(sections, blocks, group, early, written):
    own, dimension = group[0], group[0].shape[-1]
    last = blocks - 1
    count = own.shape[0] // 2

    def body(own, from_first, from_second, from_partner, *rest):
        out, total, sems = rest[-3:]
        right_half = half_of(sections)
        outer = is_at(0, sections)
        copies = []
        for k in range(count):
            low, high = (0, last) if early else (k + 1, k)
            index = jnp.where(outer, low, high)
            place = jnp.where(right_half, last - index, index)
            for part in (1, 0):
                slot = 2 * k + part
                if part:
                    total[slot] = own[slot] + from_partner[k]
                else:
                    total[slot] = own[slot] + (from_first[k] + from_second[k])
                copies.append(
                    pltpu.make_async_copy(total.at[slot], out.at[0, place, part], sems.at[slot])
                )
                copies[-1].start()
        for copy in copies:
            copy.wait()

    outside = pl.BlockSpec(memory_space=pltpu.HBM)
    before = [] if written is None else [written]
    return pl.pallas_call(
        body,
        out_shape=jax.ShapeDtypeStruct((1, blocks, 2, dimension, dimension), F32),
        in_specs=[VMEM] * 4 + [outside] * len(before),
        out_specs=outside,
        scratch_shapes=[
            pltpu.VMEM((2 * count, dimension, dimension), F32),
            pltpu.SemaphoreType.DMA((2 * count,)),
        ],
        input_output_aliases={4: 0} if before else {},
        compiler_params=pltpu.CompilerParams(vmem_limit_bytes=12 << 20),
    )(*group, *before)


def step(
    onsite, hopping, coupling, broadening, born_sigma, phonon_shift, phonon_local, phonon_side
):
    blocks = onsite.shape[0]
    sections = lax.axis_size("section")
    spread = lax.axis_size("energy")
    assert born_sigma.shape[0] == 1 and spread % 2 == 0
    assert sections % 4 == 0 and sections // 4 == 1 and blocks >= 2
    half = sections // 2
    last = blocks - 1
    pairs = [(s, s ^ 1) for s in range(sections)]
    across = [(half - 1, half), (half, half - 1)]

    def over_section(value, route):
        return lax.ppermute(value, "section", route)

    def over_energy(value, route):
        return lax.ppermute(value, "energy", route)

    swap = [(e, e ^ 1) for e in range(spread)]
    first_swap = [(e, e ^ 2) for e in range(spread) if e ^ 2 < spread]
    second_swap = [(e, ((e + 2) ^ 2) - 2) for e in range(spread)]
    second_swap = [(a, b) for a, b in second_swap if 0 <= b < spread]
    crossing = []
    for a, b in swap:
        for s, t in across + [(0, 0), (sections - 1, sections - 1)]:
            crossing.append((a * sections + s, (b if s == t else a) * sections + t))

    pack = prepare(sections, spread, broadening, onsite, hopping, coupling, born_sigma)

    def inner_link(table, index, reverse=False):
        place = 2 * blocks + 2 * index
        return [(table, place + 1, place) if reverse else (table, place, place + 1)]

    end = 4 * blocks - 2

    first = []
    sigma = None
    for step in range(half):
        entering = []
        if step > 0:
            sigma = enter_step(sections, step, 1, pack, sigma)
        for index in range(blocks):
            entering.append(sigma)
            given = [] if sigma is None else [sigma]
            leaves = index == last
            link = [(pack, end, end + 1)] if leaves else inner_link(pack, index)
            sigma = chain_step(sections, step, pack, index, given, link, leaves=leaves)
        first.append(entering)
        leaving = sigma
        if step < half - 1:
            sigma = over_section(sigma, pairs)
        else:
            sigma = lax.ppermute(sigma, ("energy", "section"), crossing)

    all_weights = weights(phonon_shift, phonon_local, phonon_side, leaving)
    local_weight, side_weight = all_weights
    pack_in = over_section(pack, pairs)
    arriving = enter_step(sections, half - 1, 0, pack, sigma)
    earlier = tuple(first[step][last] for step in range(half))
    sigma = over_section(arriving, pairs)
    ready = green_step(sections, half - 1, pack, last, earlier[1:], (arriving,), after=all_weights)
    for index in range(last, -1, -1):
        link = (
            inner_link(pack_in, index - 1, True)
            if index > 0
            else [(pack, end + 1, end), (pack_in, end, end + 1)]
        )
        after = ready if index == last else ()
        sigma = chain_step(sections, 0, pack_in, index, [sigma], link, after=after)
    green = green_step(sections, 0, pack, last, earlier[:1], (sigma,), passed=ready)
    second = (sigma, arriving)
    joined = []
    for index in range(last, 0, -1):
        joined.insert(0, green)
        link = inner_link(pack, index - 1, True)
        second = (
            chain_step(sections, None, pack, index, second, link, after=green),
        )
        earlier = tuple(first[step][index - 1] for step in range(half))
        green = green_step(
            sections, None, pack, index - 1, earlier, second, joined=joined if index == 1 else ()
        )
    real, imag = green
    partner = over_energy(real, swap)
    ahead = over_energy(imag, first_swap)
    behind = over_energy(imag, second_swap)
    middle_real = lax.ppermute(last_blocks(real, partner), ("energy", "section"), crossing)

    side_partner, side_own, middle, shared = side_terms(
        sections, side_weight, real, partner, imag, ahead, behind
    )
    middle = over_section(middle, across)
    shared = over_section(shared, pairs)
    tables = {
        "local_weight": local_weight,
        "side_weight": side_weight,
        "real": real,
        "partner": partner,
        "imag": imag,
        "ahead": ahead,
        "behind": behind,
        "side_partner": side_partner,
        "side_own": side_own,
    }

    def exchange(to_first, to_second, to_partner, own):
        from_first = over_energy(to_first, first_swap)
        from_second = over_energy(to_second, second_swap)
        from_partner = over_energy(to_partner, swap)
        return own, from_first, from_second, from_partner

    ends = {"middle_real": middle_real, "middle": middle}
    early = combine(sections, tables | ends, True)
    early = exchange(*early)
    late = combine(sections, tables | {"shared": shared}, False)
    late = exchange(*late)
    result = finish(sections, blocks, early, True, None)
    return finish(sections, blocks, late, False, result)


def solution(mesh):
    in_specs = (
        P("section", None),
        P("section", None, None),
        P("section", None, None),
        P("energy"),
        P("energy", "section", None, None, None),
        P(),
        P(),
        P(),
    )
    out_specs = P("energy", "section", None, None, None)
    return jax.shard_map(step, mesh=mesh, in_specs=in_specs, out_specs=out_specs, check_vma=False)
```

```python
import functools

import jax
import jax.numpy as jnp
from jax import lax
from jax.experimental import pallas as pl
from jax.experimental.pallas import tpu as pltpu
from jax.sharding import PartitionSpec as P


F32 = jnp.float32
BF16 = jnp.bfloat16
VMEM = pl.BlockSpec(memory_space=pltpu.VMEM)


def split(value):
    high = value.astype(BF16)
    return high, (value - high.astype(F32)).astype(BF16)


def product(left, right):
    def dot(a, b):
        return jnp.dot(a, b, preferred_element_type=F32)

    return dot(left[0], right[0]) + (dot(left[0], right[1]) + dot(left[1], right[0]))


def parts(real, imag):
    return split(real), split(imag), split(real + imag)


def complex_product(left, right):
    first = product(left[0], right[0])
    second = product(left[1], right[1])
    third = product(left[2], right[2])
    return first - second, third - (first + second)


def start_series(real, imag):
    shape = real.shape
    eye = lax.broadcasted_iota(jnp.int32, shape, 0) == lax.broadcasted_iota(jnp.int32, shape, 1)
    a = jnp.sum(jnp.where(eye, real, 0.0), 0, keepdims=True)
    b = jnp.sum(jnp.where(eye, imag, 0.0), 0, keepdims=True)
    modulus = a * a + b * b
    col_real, col_imag = a / modulus, -b / modulus
    row_real, row_imag = col_real.reshape(-1, 1), col_imag.reshape(-1, 1)
    e_real = jnp.where(eye, 0.0, imag * col_imag - real * col_real)
    e_imag = jnp.where(eye, 0.0, -(real * col_imag + imag * col_real))
    t_real = e_real + jnp.where(eye, 1.0, 0.0)
    x_real = row_real * t_real - row_imag * e_imag
    x_imag = row_real * e_imag + row_imag * t_real
    return e_real, e_imag, x_real, x_imag


def series_square(real, imag):
    e_real, e_imag, x_real, x_imag = start_series(real, imag)
    e_parts = parts(e_real, e_imag)
    return x_real, x_imag, parts(*complex_product(e_parts, e_parts))


def half_of(sections):
    return lax.axis_index("section") >= sections // 2


def is_at(step, sections):
    slot = lax.axis_index("section")
    return jnp.logical_or(slot == step, slot == sections - 1 - step)


def chain_core(real, imag, link, link_t, out):
    x_real, x_imag, f_parts = series_square(real, imag)
    right = split(link)
    left = split(link_t)
    a_real = product(left, split(x_real))
    a_imag = product(left, split(x_imag))
    b_real, b_imag = complex_product(parts(a_real, a_imag), f_parts)
    g_real, g_imag = complex_product(f_parts, f_parts)
    w_real = product(split(g_real), right) + link
    w_imag = product(split(g_imag), right)
    s_real, s_imag = complex_product(parts(b_real + a_real, b_imag + a_imag), parts(w_real, w_imag))
    out[0] = s_real
    out[1] = s_imag


def inverse_core(real, imag, put):
    x_real, x_imag, f_parts = series_square(real, imag)
    b_real, b_imag = complex_product(parts(x_real, x_imag), f_parts)
    g_real, g_imag = complex_product(f_parts, f_parts)
    b_real = b_real + x_real
    b_imag = b_imag + x_imag
    s_real, s_imag = complex_product(parts(b_real, b_imag), parts(g_real, g_imag))
    put(0, b_real + s_real)
    put(1, b_imag + s_imag)


def call(body, out_shape, operands, products):
    dimension = operands[0].shape[-1]
    size = dimension * dimension
    return pl.pallas_call(
        body,
        out_shape=out_shape,
        in_specs=[VMEM] * len(operands),
        out_specs=jax.tree.map(lambda _: VMEM, out_shape),
        compiler_params=pltpu.CompilerParams(vmem_limit_bytes=12 << 20),
        cost_estimate=pl.CostEstimate(
            flops=6 * products * size * dimension, bytes_accessed=4 * 8 * size, transcendentals=0
        ),
    )(*operands)


def enter_step(sections, active, coupled_half, pack, given):
    place = pack.shape[0] - 2

    def body(source, value, out):
        mine = is_at(active, sections)
        coupled = half_of(sections) if coupled_half else jnp.logical_not(half_of(sections))

        @pl.when(jnp.logical_and(mine, coupled))
        def _():
            link, link_t = split(source[place]), split(source[place + 1])
            for part in (0, 1):
                out[part] = product(split(product(link, split(value[part]))), link_t)

        @pl.when(jnp.logical_not(jnp.logical_and(mine, coupled)))
        def _():
            out[...] = value[...]

    return call(body, jax.ShapeDtypeStruct(given.shape, F32), [pack, given], 4)


def link_ways(sections, refs, links):
    ways = [(ref[link[1]], ref[link[2]]) for ref, link in zip(refs, links)]
    if len(ways) == 1:
        return ways[0]
    right_half = half_of(sections)
    return tuple(jnp.where(right_half, b, a) for a, b in zip(*ways))


def chain_step(sections, active, pack, block, sigmas, links, after=(), leaves=False):
    arrays = [pack] + list(sigmas) + [link[0] for link in links]
    count = len(arrays)

    def body(*refs):
        out = refs[-1]
        source = refs[0]
        given = refs[1 : 1 + len(sigmas)]

        def work():
            real, imag = source[2 * block], source[2 * block + 1]
            if len(given) == 1:
                real, imag = real - given[0][0], imag - given[0][1]
            elif len(given) == 2:
                outer = is_at(0, sections)
                real = real - jnp.where(outer, given[0][0], given[1][0])
                imag = imag - jnp.where(outer, given[0][1], given[1][1])
            link, link_t = link_ways(sections, refs[1 + len(sigmas) : count], links)
            if not leaves:
                chain_core(real, imag, link, link_t, out)
                return

            def put(place, value):
                out[place] = value

            right_half = half_of(sections)
            pl.when(right_half)(lambda: inverse_core(real, imag, put))
            pl.when(jnp.logical_not(right_half))(
                lambda: chain_core(real, imag, link, link_t, out)
            )

        if active is None:
            work()
        else:
            mine = is_at(active, sections)
            pl.when(mine)(work)

            @pl.when(jnp.logical_not(mine))
            def _():
                out[...] = jnp.zeros_like(out)

    shape = jax.ShapeDtypeStruct((2,) + pack.shape[1:], F32)
    return call(body, shape, arrays + list(after), 16)


def green_value(source, block, terms):
    value = [source[2 * block], source[2 * block + 1]]
    for place in (0, 1):
        for term in terms:
            value[place] = value[place] - term(place)
    return value


def green_step(sections, active, pack, block, sigmas, after=()):
    arrays = [pack] + list(sigmas)

    def body(*refs):
        outs = refs[-2:]

        def put(place, value):
            outs[place][...] = value

        def work():
            terms = [lambda place, ref=ref: ref[place] for ref in refs[1 : len(arrays)]]
            inverse_core(*green_value(refs[0], block, terms), put)

        if active is None:
            work()
            return
        mine = is_at(active, sections)
        pl.when(mine)(work)

        @pl.when(jnp.logical_not(mine))
        def _():
            for place in (0, 1):
                put(place, jnp.zeros(refs[0].shape[1:], F32))

    flat = jax.ShapeDtypeStruct(pack.shape[1:], F32)
    return call(body, (flat, flat), arrays + list(after), 12)


def greens_at_ends(sections, pack, outer_terms, ready, inner_first, second, between):
    last = len(between) + 1
    flat_between = [a for pair in between for a in pair]
    arrays = [pack, *outer_terms, *ready, inner_first, second, *flat_between]
    count = len(outer_terms)

    def body(*refs):
        outs = refs[-2:]
        source = refs[0]
        extra = refs[1 : 1 + count]
        done = refs[1 + count : 3 + count]
        inner_sigma, sigma = refs[3 + count : 5 + count]
        rest = refs[5 + count : -2]
        outer = is_at(0, sections)

        def at(ref):
            return lambda place: ref[place]

        def put_at(index):
            def put(place, value):
                outs[place][index] = value

            return put

        @pl.when(outer)
        def _():
            inverse_core(*green_value(source, last, [at(ref) for ref in extra]), put_at(last))
            inverse_core(*green_value(source, 0, [at(sigma)]), put_at(0))

        @pl.when(jnp.logical_not(outer))
        def _():
            inverse_core(*green_value(source, 0, [at(inner_sigma), at(sigma)]), put_at(0))
            for place in (0, 1):
                outs[place][last] = done[place][...]

        for number in range(last - 1):
            for place in (0, 1):
                outs[place][1 + number] = rest[2 * number + place][...]

    stack = jax.ShapeDtypeStruct((last + 1,) + pack.shape[1:], F32)
    return call(body, (stack, stack), arrays, 24)


def prepare_kernel(
    sections, spread, broadening, onsite, hopping, coupling, born, pack, hop, cup, sig, levels, sems
):
    blocks, dimension = onsite.shape
    copies = []
    for index in range(blocks):
        for order, (source, target) in enumerate(
            (
                (hopping.at[index], hop.at[index]),
                (born.at[0, index], sig.at[index]),
                (coupling.at[index], cup.at[index]),
            )
        ):
            copy = pltpu.make_async_copy(source, target, sems.at[3 * index + order])
            copy.start()
            copies.append(copy)
    copies.append(pltpu.make_async_copy(onsite, levels, sems.at[3 * blocks]))
    copies[-1].start()
    right_half = half_of(sections)
    flip = right_half.astype(jnp.int32)
    shape = (dimension, dimension)
    eye = lax.broadcasted_iota(jnp.int32, shape, 0) == lax.broadcasted_iota(jnp.int32, shape, 1)
    position = lax.axis_index("energy").astype(F32)
    energy = -2.0 + position * (4.0 / (spread - 1))
    copies[3 * blocks].wait()
    width = jnp.broadcast_to(broadening[...], shape)
    for index in range(blocks):
        place = jnp.where(right_half, blocks - 1 - index, index)
        copies[3 * index].wait()
        block = hop[index]
        level = energy - levels[pl.ds(index, 1), :]
        real = jnp.where(eye, jnp.broadcast_to(level, shape), 0.0) - 0.5 * (block + block.T)
        copies[3 * index + 1].wait()
        pack[2 * place] = real - sig[index, 0]
        pack[2 * place + 1] = jnp.where(eye, width, 0.0) - sig[index, 1]
        copies[3 * index + 2].wait()
        link = cup[index]
        if index < blocks - 1:
            place = 2 * blocks + 2 * jnp.where(right_half, blocks - 2 - index, index)
            pack[place + flip] = link
            pack[place + 1 - flip] = link.T
        else:
            pack[4 * blocks - 2] = link
            pack[4 * blocks - 1] = link.T


def prepare(sections, spread, broadening, onsite, hopping, coupling, born):
    blocks, dimension = onsite.shape
    outside = pl.BlockSpec(memory_space=pltpu.HBM)
    return pl.pallas_call(
        functools.partial(prepare_kernel, sections, spread),
        out_shape=jax.ShapeDtypeStruct((4 * blocks, dimension, dimension), F32),
        in_specs=[VMEM] + [outside] * 4,
        out_specs=VMEM,
        scratch_shapes=[
            pltpu.VMEM((blocks, dimension, dimension), F32),
            pltpu.VMEM((blocks, dimension, dimension), F32),
            pltpu.VMEM((blocks, 2, dimension, dimension), F32),
            pltpu.VMEM((blocks, dimension), F32),
            pltpu.SemaphoreType.DMA((3 * blocks + 1,)),
        ],
        compiler_params=pltpu.CompilerParams(vmem_limit_bytes=16 << 20),
        name="prepare",
    )(
        broadening.reshape(1, 1),
        *(
            pltpu.with_memory_space_constraint(value, pltpu.HBM)
            for value in (onsite, hopping, coupling, born)
        )
    )


OWN, NEXT, OTHER, PAIR, LONE = range(5)


def is_even():
    return lax.axis_index("energy") % 2 == 0


def first_is_far():
    slot = lax.axis_index("energy")
    return (slot // 2) % 2 == slot % 2


def weights(shifts, local_weight, side_weight, after):
    shape = jax.ShapeDtypeStruct((5,) + local_weight.shape[1:], F32)

    def body(shift_ref, local_ref, side_ref, _, local_out, side_out):
        even = is_even()
        low, high = jnp.where(even, NEXT, OTHER), jnp.where(even, OTHER, NEXT)
        far_low, far_high = jnp.where(even, PAIR, LONE), jnp.where(even, LONE, PAIR)
        for source, target in ((local_ref, local_out), (side_ref, side_out)):
            for shift, place in ((0, OWN), (-1, low), (1, high), (-2, far_low), (2, far_high)):
                total = jnp.zeros(source.shape[1:], F32)
                for mode in range(source.shape[0]):
                    total = total + jnp.where(shift_ref[mode] == shift, source[mode], 0.0)
                target[place] = total

    return pl.pallas_call(
        body,
        out_shape=(shape, shape),
        in_specs=[pl.BlockSpec(memory_space=pltpu.SMEM)] + [VMEM] * 3,
        out_specs=(VMEM, VMEM),
        compiler_params=pltpu.CompilerParams(vmem_limit_bytes=12 << 20),
        cost_estimate=pl.CostEstimate(flops=1 << 20, bytes_accessed=8 << 20, transcendentals=0),
        name="weights",
    )(shifts, local_weight, side_weight, after)


def last_blocks(*tables):
    last = tables[0].shape[0] - 1

    def body(*refs):
        for place, ref in enumerate(refs[:-1]):
            refs[-1][place] = ref[last]

    shape = jax.ShapeDtypeStruct((len(tables),) + tables[0].shape[1:], F32)
    return call(body, shape, list(tables), 1)


def side_terms(sections, side_weight, real, partner, imag, ahead, behind):
    blocks, dimension = real.shape[0], real.shape[-1]
    flat = (dimension, dimension)

    def body(weight, real, partner, imag, ahead, behind, for_partner, own, middle, shared):
        outer = is_at(0, sections)
        chosen = first_is_far()
        for index in range(blocks):
            far = jnp.where(chosen, ahead[index], behind[index])
            near = jnp.where(chosen, behind[index], ahead[index])
            value = imag[index]
            for_partner[index] = weight[NEXT] * value + weight[OTHER] * far
            own[index] = weight[OWN] * value + weight[LONE] * far + weight[PAIR] * near
        last = blocks - 1
        middle[0] = for_partner[last]
        middle[1] = own[last]
        for place, table in enumerate((real, partner, for_partner, own)):
            shared[place] = jnp.where(outer, table[last], table[0])

    def shape(count):
        return jax.ShapeDtypeStruct((count,) + flat, F32)

    return call(
        body,
        (shape(blocks), shape(blocks), shape(2), shape(4)),
        [side_weight, real, partner, imag, ahead, behind],
        1,
    )


def combine(sections, tables, early):
    names = list(tables)
    blocks, dimension = tables["real"].shape[0], tables["real"].shape[-1]
    last = blocks - 1
    count = 1 if early else last

    def body(*refs):
        t = dict(zip(names, refs))
        to_first, to_second, to_partner, own = refs[len(names) :]
        a, b = t["local_weight"], t["side_weight"]
        chosen = first_is_far()

        def emit(place, index, ends):
            sides = []
            for number, name in enumerate(("real", "partner", "side_partner", "side_own")):
                terms = [t[name][i] for i in (index - 1, index + 1) if 0 <= i <= last]
                terms += [end(number) for end in ends]
                sides.append(functools.reduce(jnp.add, terms))
            n_real, n_partner, n_for, n_own = sides
            real, partner, imag = t["real"][index], t["partner"][index], t["imag"][index]
            ahead, behind = t["ahead"][index], t["behind"][index]
            far = jnp.where(chosen, ahead, behind)
            near = jnp.where(chosen, behind, ahead)
            pair = a[PAIR] * real + a[NEXT] * partner + b[PAIR] * n_real + b[NEXT] * n_partner
            lone = a[LONE] * real + b[LONE] * n_real
            to_first[place] = jnp.where(chosen, pair, lone)
            to_second[place] = jnp.where(chosen, lone, pair)
            to_partner[place] = a[NEXT] * imag + a[OTHER] * far + n_for
            own[2 * place] = (
                a[OWN] * real + a[OTHER] * partner + b[OWN] * n_real + b[OTHER] * n_partner
            )
            own[2 * place + 1] = a[OWN] * imag + a[LONE] * far + a[PAIR] * near + n_own

        def middle(number):
            return t["middle_real"][number] if number < 2 else t["middle"][number - 2]

        def shared(number):
            return t["shared"][number]

        outer = is_at(0, sections)

        @pl.when(outer)
        def _():
            for place in range(count):
                index = 0 if early else place + 1
                emit(place, index, [shared] if not early and index == last else [])

        @pl.when(jnp.logical_not(outer))
        def _():
            for place in range(count):
                index = last if early else place
                emit(place, index, [middle] if early else [shared] if index == 0 else [])

    def shape(count):
        return jax.ShapeDtypeStruct((count, dimension, dimension), F32)

    return call(
        body,
        (shape(count), shape(count), shape(count), shape(2 * count)),
        [tables[name] for name in names],
        1,
    )


def finish(sections, blocks, group, early, written):
    own, dimension = group[0], group[0].shape[-1]
    last = blocks - 1
    count = own.shape[0] // 2

    def body(own, from_first, from_second, from_partner, *rest):
        out, total, sems = rest[-3:]
        right_half = half_of(sections)
        outer = is_at(0, sections)
        copies = []
        for k in range(count):
            low, high = (0, last) if early else (k + 1, k)
            index = jnp.where(outer, low, high)
            place = jnp.where(right_half, last - index, index)
            for part in (1, 0):
                slot = 2 * k + part
                if part:
                    total[slot] = own[slot] + from_partner[k]
                else:
                    total[slot] = own[slot] + (from_first[k] + from_second[k])
                copies.append(
                    pltpu.make_async_copy(total.at[slot], out.at[0, place, part], sems.at[slot])
                )
                copies[-1].start()
        for copy in copies:
            copy.wait()

    outside = pl.BlockSpec(memory_space=pltpu.HBM)
    before = [] if written is None else [written]
    return pl.pallas_call(
        body,
        out_shape=jax.ShapeDtypeStruct((1, blocks, 2, dimension, dimension), F32),
        in_specs=[VMEM] * 4 + [outside] * len(before),
        out_specs=outside,
        scratch_shapes=[
            pltpu.VMEM((2 * count, dimension, dimension), F32),
            pltpu.SemaphoreType.DMA((2 * count,)),
        ],
        input_output_aliases={4: 0} if before else {},
        compiler_params=pltpu.CompilerParams(vmem_limit_bytes=12 << 20),
    )(*group, *before)


def chosen_first(sections, outer_value, inner_value):
    return jnp.where(is_at(0, sections), outer_value, inner_value)


def step(
    onsite, hopping, coupling, broadening, born_sigma, phonon_shift, phonon_local, phonon_side
):
    blocks = onsite.shape[0]
    sections = lax.axis_size("section")
    spread = lax.axis_size("energy")
    assert born_sigma.shape[0] == 1 and spread % 2 == 0
    assert sections % 4 == 0 and sections // 4 == 1 and blocks >= 2
    half = sections // 2
    last = blocks - 1
    pairs = [(s, s ^ 1) for s in range(sections)]
    across = [(half - 1, half), (half, half - 1)]

    def over_section(value, route):
        return lax.ppermute(value, "section", route)

    def over_energy(value, route):
        return lax.ppermute(value, "energy", route)

    swap = [(e, e ^ 1) for e in range(spread)]
    first_swap = [(e, e ^ 2) for e in range(spread) if e ^ 2 < spread]
    second_swap = [(e, ((e + 2) ^ 2) - 2) for e in range(spread)]
    second_swap = [(a, b) for a, b in second_swap if 0 <= b < spread]
    crossing = []
    for a, b in swap:
        for s, t in across + [(0, 0), (sections - 1, sections - 1)]:
            crossing.append((a * sections + s, (b if s == t else a) * sections + t))

    pack = prepare(sections, spread, broadening, onsite, hopping, coupling, born_sigma)

    def inner_link(table, index, reverse=False):
        place = 2 * blocks + 2 * index
        return [(table, place + 1, place) if reverse else (table, place, place + 1)]

    end = 4 * blocks - 2

    first = []
    sigma = None
    for step in range(half):
        entering = []
        if step > 0:
            sigma = enter_step(sections, step, 1, pack, sigma)
        for index in range(blocks):
            entering.append(sigma)
            given = [] if sigma is None else [sigma]
            leaves = index == last
            link = [(pack, end, end + 1)] if leaves else inner_link(pack, index)
            sigma = chain_step(sections, step, pack, index, given, link, leaves=leaves)
        first.append(entering)
        leaving = sigma
        if step < half - 1:
            sigma = over_section(sigma, pairs)
        else:
            sigma = lax.ppermute(sigma, ("energy", "section"), crossing)

    all_weights = weights(phonon_shift, phonon_local, phonon_side, leaving)
    local_weight, side_weight = all_weights
    pack_in = over_section(pack, pairs)
    arriving = enter_step(sections, half - 1, 0, pack, sigma)
    earlier = tuple(first[step][last] for step in range(half))
    sigma = over_section(arriving, pairs)
    ready = green_step(
        sections, half - 1, pack, last, (first[half - 1][last], arriving), after=all_weights
    )
    for index in range(last, -1, -1):
        link = (
            inner_link(pack_in, index - 1, True)
            if index > 0
            else [(pack, end + 1, end), (pack_in, end, end + 1)]
        )
        after = ready if index == last else ()
        sigma = chain_step(sections, 0, pack_in, index, [sigma], link, after=after)
    entered = (sigma, arriving)
    between = []
    for index in range(last, 0, -1):
        link = inner_link(pack, index - 1, True)
        sent = chain_step(sections, None, pack, index, entered, link, after=ready)
        entered = (sent,)
        if index > 1:
            kept = chosen_first(sections, *(first[step][index - 1] for step in range(half)))
            between.insert(0, green_step(sections, None, pack, index - 1, (kept, sent)))
    real, imag = greens_at_ends(
        sections, pack, (first[0][last], sigma), ready, first[half - 1][0], entered[0], between
    )
    partner = over_energy(real, swap)
    ahead = over_energy(imag, first_swap)
    behind = over_energy(imag, second_swap)
    middle_real = over_section(last_blocks(real, partner), across)

    side_partner, side_own, middle, shared = side_terms(
        sections, side_weight, real, partner, imag, ahead, behind
    )
    middle = over_section(middle, across)
    shared = over_section(shared, pairs)
    tables = {
        "local_weight": local_weight,
        "side_weight": side_weight,
        "real": real,
        "partner": partner,
        "imag": imag,
        "ahead": ahead,
        "behind": behind,
        "side_partner": side_partner,
        "side_own": side_own,
    }

    def exchange(to_first, to_second, to_partner, own):
        from_first = over_energy(to_first, first_swap)
        from_second = over_energy(to_second, second_swap)
        from_partner = over_energy(to_partner, swap)
        return own, from_first, from_second, from_partner

    ends = {"middle_real": middle_real, "middle": middle}
    early = combine(sections, tables | ends, True)
    early = exchange(*early)
    late = combine(sections, tables | {"shared": shared}, False)
    late = exchange(*late)
    result = finish(sections, blocks, early, True, None)
    return finish(sections, blocks, late, False, result)


def solution(mesh):
    in_specs = (
        P("section", None),
        P("section", None, None),
        P("section", None, None),
        P("energy"),
        P("energy", "section", None, None, None),
        P(),
        P(),
        P(),
    )
    out_specs = P("energy", "section", None, None, None)
    return jax.shard_map(step, mesh=mesh, in_specs=in_specs, out_specs=out_specs, check_vma=False)
```

```python
import functools

import jax
import jax.numpy as jnp
from jax import lax
from jax.experimental import pallas as pl
from jax.experimental.pallas import tpu as pltpu
from jax.sharding import PartitionSpec as P


F32 = jnp.float32
BF16 = jnp.bfloat16
VMEM = pl.BlockSpec(memory_space=pltpu.VMEM)


def split(value):
    high = value.astype(BF16)
    return high, (value - high.astype(F32)).astype(BF16)


def product(left, right):
    def dot(a, b):
        return jnp.dot(a, b, preferred_element_type=F32)

    return dot(left[0], right[0]) + (dot(left[0], right[1]) + dot(left[1], right[0]))


def parts(real, imag):
    return split(real), split(imag), split(real + imag)


def complex_product(left, right):
    first = product(left[0], right[0])
    second = product(left[1], right[1])
    third = product(left[2], right[2])
    return first - second, third - (first + second)


def start_series(real, imag):
    shape = real.shape
    eye = lax.broadcasted_iota(jnp.int32, shape, 0) == lax.broadcasted_iota(jnp.int32, shape, 1)
    a = jnp.sum(jnp.where(eye, real, 0.0), 0, keepdims=True)
    b = jnp.sum(jnp.where(eye, imag, 0.0), 0, keepdims=True)
    modulus = a * a + b * b
    col_real, col_imag = a / modulus, -b / modulus
    row_real, row_imag = col_real.reshape(-1, 1), col_imag.reshape(-1, 1)
    e_real = jnp.where(eye, 0.0, imag * col_imag - real * col_real)
    e_imag = jnp.where(eye, 0.0, -(real * col_imag + imag * col_real))
    t_real = e_real + jnp.where(eye, 1.0, 0.0)
    x_real = row_real * t_real - row_imag * e_imag
    x_imag = row_real * e_imag + row_imag * t_real
    return e_real, e_imag, x_real, x_imag


def series_square(real, imag):
    e_real, e_imag, x_real, x_imag = start_series(real, imag)
    e_parts = parts(e_real, e_imag)
    return x_real, x_imag, parts(*complex_product(e_parts, e_parts))


def half_of(sections):
    return lax.axis_index("section") >= sections // 2


def is_at(step, sections):
    slot = lax.axis_index("section")
    return jnp.logical_or(slot == step, slot == sections - 1 - step)


def chain_core(real, imag, link, link_t, out):
    x_real, x_imag, f_parts = series_square(real, imag)
    right = split(link)
    left = split(link_t)
    a_real = product(left, split(x_real))
    a_imag = product(left, split(x_imag))
    b_real, b_imag = complex_product(parts(a_real, a_imag), f_parts)
    g_real, g_imag = complex_product(f_parts, f_parts)
    w_real = product(split(g_real), right) + link
    w_imag = product(split(g_imag), right)
    s_real, s_imag = complex_product(parts(b_real + a_real, b_imag + a_imag), parts(w_real, w_imag))
    out[0] = s_real
    out[1] = s_imag


def inverse_core(real, imag, put):
    x_real, x_imag, f_parts = series_square(real, imag)
    b_real, b_imag = complex_product(parts(x_real, x_imag), f_parts)
    g_real, g_imag = complex_product(f_parts, f_parts)
    b_real = b_real + x_real
    b_imag = b_imag + x_imag
    s_real, s_imag = complex_product(parts(b_real, b_imag), parts(g_real, g_imag))
    put(0, b_real + s_real)
    put(1, b_imag + s_imag)


def call(body, out_shape, operands, products):
    dimension = operands[0].shape[-1]
    size = dimension * dimension
    return pl.pallas_call(
        body,
        out_shape=out_shape,
        in_specs=[VMEM] * len(operands),
        out_specs=jax.tree.map(lambda _: VMEM, out_shape),
        compiler_params=pltpu.CompilerParams(vmem_limit_bytes=12 << 20),
        cost_estimate=pl.CostEstimate(
            flops=6 * products * size * dimension, bytes_accessed=4 * 8 * size, transcendentals=0
        ),
    )(*operands)


def enter_step(sections, active, coupled_half, pack, given):
    place = pack.shape[0] - 2

    def body(source, value, out):
        mine = is_at(active, sections)
        coupled = half_of(sections) if coupled_half else jnp.logical_not(half_of(sections))

        @pl.when(jnp.logical_and(mine, coupled))
        def _():
            link, link_t = split(source[place]), split(source[place + 1])
            for part in (0, 1):
                out[part] = product(split(product(link, split(value[part]))), link_t)

        @pl.when(jnp.logical_not(jnp.logical_and(mine, coupled)))
        def _():
            out[...] = value[...]

    return call(body, jax.ShapeDtypeStruct(given.shape, F32), [pack, given], 4)


def link_ways(sections, refs, links):
    ways = [(ref[link[1]], ref[link[2]]) for ref, link in zip(refs, links)]
    if len(ways) == 1:
        return ways[0]
    right_half = half_of(sections)
    return tuple(jnp.where(right_half, b, a) for a, b in zip(*ways))


def chain_step(sections, active, pack, block, sigmas, links, after=(), leaves=False):
    arrays = [pack] + list(sigmas) + [link[0] for link in links]
    count = len(arrays)

    def body(*refs):
        out = refs[-1]
        source = refs[0]
        given = refs[1 : 1 + len(sigmas)]

        def work():
            real, imag = source[2 * block], source[2 * block + 1]
            if len(given) == 1:
                real, imag = real - given[0][0], imag - given[0][1]
            elif len(given) == 2:
                outer = is_at(0, sections)
                real = real - jnp.where(outer, given[0][0], given[1][0])
                imag = imag - jnp.where(outer, given[0][1], given[1][1])
            link, link_t = link_ways(sections, refs[1 + len(sigmas) : count], links)
            if not leaves:
                chain_core(real, imag, link, link_t, out)
                return

            def put(place, value):
                out[place] = value

            right_half = half_of(sections)
            pl.when(right_half)(lambda: inverse_core(real, imag, put))
            pl.when(jnp.logical_not(right_half))(
                lambda: chain_core(real, imag, link, link_t, out)
            )

        if active is None:
            work()
        else:
            mine = is_at(active, sections)
            pl.when(mine)(work)

            @pl.when(jnp.logical_not(mine))
            def _():
                out[...] = jnp.zeros_like(out)

    shape = jax.ShapeDtypeStruct((2,) + pack.shape[1:], F32)
    return call(body, shape, arrays + list(after), 16)


def green_value(source, block, terms):
    value = [source[2 * block], source[2 * block + 1]]
    for place in (0, 1):
        for term in terms:
            value[place] = value[place] - term(place)
    return value


def green_step(sections, active, pack, block, sigmas, after=()):
    arrays = [pack] + list(sigmas)

    def body(*refs):
        outs = refs[-2:]

        def put(place, value):
            outs[place][...] = value

        def work():
            terms = [lambda place, ref=ref: ref[place] for ref in refs[1 : len(arrays)]]
            inverse_core(*green_value(refs[0], block, terms), put)

        if active is None:
            work()
            return
        mine = is_at(active, sections)
        pl.when(mine)(work)

        @pl.when(jnp.logical_not(mine))
        def _():
            for place in (0, 1):
                put(place, jnp.zeros(refs[0].shape[1:], F32))

    flat = jax.ShapeDtypeStruct(pack.shape[1:], F32)
    return call(body, (flat, flat), arrays + list(after), 12)


def greens_at_ends(sections, pack, outer_terms, ready, inner_first, second, between):
    last = len(between) + 1
    flat_between = [a for pair in between for a in pair]
    arrays = [pack, *outer_terms, *ready, inner_first, second, *flat_between]
    count = len(outer_terms)

    def body(*refs):
        outs = refs[-2:]
        source = refs[0]
        extra = refs[1 : 1 + count]
        done = refs[1 + count : 3 + count]
        inner_sigma, sigma = refs[3 + count : 5 + count]
        rest = refs[5 + count : -2]
        outer = is_at(0, sections)

        def at(ref):
            return lambda place: ref[place]

        def put_at(index):
            def put(place, value):
                outs[place][index] = value

            return put

        @pl.when(outer)
        def _():
            inverse_core(*green_value(source, last, [at(ref) for ref in extra]), put_at(last))
            inverse_core(*green_value(source, 0, [at(sigma)]), put_at(0))

        @pl.when(jnp.logical_not(outer))
        def _():
            inverse_core(*green_value(source, 0, [at(inner_sigma), at(sigma)]), put_at(0))
            for place in (0, 1):
                outs[place][last] = done[place][...]

        for number in range(last - 1):
            for place in (0, 1):
                outs[place][1 + number] = rest[2 * number + place][...]

    stack = jax.ShapeDtypeStruct((last + 1,) + pack.shape[1:], F32)
    return call(body, (stack, stack), arrays, 24)


def prepare_kernel(
    sections, spread, broadening, onsite, hopping, coupling, born, pack, first, hop, cup, sig, levels, sems
):
    blocks, dimension = onsite.shape
    right_half = half_of(sections)
    local_of = [jnp.where(right_half, blocks - 1 - k, k) for k in range(blocks)]
    link_of = [jnp.where(right_half, blocks - 2 - k, k) for k in range(blocks - 1)] + [blocks - 1]
    levels_copy = pltpu.make_async_copy(onsite, levels, sems.at[3 * blocks])
    levels_copy.start()
    copies = []
    for index in range(blocks):
        for order, (source, target) in enumerate(
            (
                (hopping.at[local_of[index]], hop.at[index]),
                (born.at[0, local_of[index]], sig.at[index]),
                (coupling.at[link_of[index]], cup.at[index]),
            )
        ):
            copy = pltpu.make_async_copy(source, target, sems.at[3 * index + order])
            copy.start()
            copies.append(copy)
    flip = right_half.astype(jnp.int32)
    shape = (dimension, dimension)
    eye = lax.broadcasted_iota(jnp.int32, shape, 0) == lax.broadcasted_iota(jnp.int32, shape, 1)
    position = lax.axis_index("energy").astype(F32)
    energy = -2.0 + position * (4.0 / (spread - 1))
    levels_copy.wait()
    width = jnp.broadcast_to(broadening[...], shape)
    for index in range(blocks):
        copies[3 * index].wait()
        block = hop[index]
        level = energy - levels[pl.ds(local_of[index], 1), :]
        real = jnp.where(eye, jnp.broadcast_to(level, shape), 0.0) - 0.5 * (block + block.T)
        copies[3 * index + 1].wait()
        pack[2 * index] = real - sig[index, 0]
        pack[2 * index + 1] = jnp.where(eye, width, 0.0) - sig[index, 1]
        copies[3 * index + 2].wait()
        link = cup[index]
        place = 2 * blocks + 2 * index
        if index == blocks - 1:
            pack[place] = link
            pack[place + 1] = link.T
        else:
            pack[place + flip] = link
            pack[place + 1 - flip] = link.T
        if index == 0:
            active = is_at(0, sections)

            @pl.when(active)
            def _():
                chain_core(pack[0], pack[1], pack[2 * blocks], pack[2 * blocks + 1], first)

            @pl.when(jnp.logical_not(active))
            def _():
                first[...] = jnp.zeros_like(first)


def prepare(sections, spread, broadening, onsite, hopping, coupling, born):
    blocks, dimension = onsite.shape
    outside = pl.BlockSpec(memory_space=pltpu.HBM)
    return pl.pallas_call(
        functools.partial(prepare_kernel, sections, spread),
        out_shape=(
            jax.ShapeDtypeStruct((4 * blocks, dimension, dimension), F32),
            jax.ShapeDtypeStruct((2, dimension, dimension), F32),
        ),
        in_specs=[VMEM] + [outside] * 4,
        out_specs=(VMEM, VMEM),
        scratch_shapes=[
            pltpu.VMEM((blocks, dimension, dimension), F32),
            pltpu.VMEM((blocks, dimension, dimension), F32),
            pltpu.VMEM((blocks, 2, dimension, dimension), F32),
            pltpu.VMEM((blocks, dimension), F32),
            pltpu.SemaphoreType.DMA((3 * blocks + 1,)),
        ],
        compiler_params=pltpu.CompilerParams(vmem_limit_bytes=16 << 20),
        name="prepare",
    )(
        broadening.reshape(1, 1),
        *(
            pltpu.with_memory_space_constraint(value, pltpu.HBM)
            for value in (onsite, hopping, coupling, born)
        )
    )


OWN, NEXT, OTHER, PAIR, LONE = range(5)


def is_even():
    return lax.axis_index("energy") % 2 == 0


def first_is_far():
    slot = lax.axis_index("energy")
    return (slot // 2) % 2 == slot % 2


def weights(shifts, local_weight, side_weight, after):
    shape = jax.ShapeDtypeStruct((5,) + local_weight.shape[1:], F32)

    def body(shift_ref, local_ref, side_ref, _, local_out, side_out):
        even = is_even()
        low, high = jnp.where(even, NEXT, OTHER), jnp.where(even, OTHER, NEXT)
        far_low, far_high = jnp.where(even, PAIR, LONE), jnp.where(even, LONE, PAIR)
        for source, target in ((local_ref, local_out), (side_ref, side_out)):
            for shift, place in ((0, OWN), (-1, low), (1, high), (-2, far_low), (2, far_high)):
                total = jnp.zeros(source.shape[1:], F32)
                for mode in range(source.shape[0]):
                    total = total + jnp.where(shift_ref[mode] == shift, source[mode], 0.0)
                target[place] = total

    return pl.pallas_call(
        body,
        out_shape=(shape, shape),
        in_specs=[pl.BlockSpec(memory_space=pltpu.SMEM)] + [VMEM] * 3,
        out_specs=(VMEM, VMEM),
        compiler_params=pltpu.CompilerParams(vmem_limit_bytes=12 << 20),
        cost_estimate=pl.CostEstimate(flops=1 << 20, bytes_accessed=8 << 20, transcendentals=0),
        name="weights",
    )(shifts, local_weight, side_weight, after)


def last_blocks(*tables):
    last = tables[0].shape[0] - 1

    def body(*refs):
        for place, ref in enumerate(refs[:-1]):
            refs[-1][place] = ref[last]

    shape = jax.ShapeDtypeStruct((len(tables),) + tables[0].shape[1:], F32)
    return call(body, shape, list(tables), 1)


def side_terms(sections, side_weight, real, partner, imag, ahead, behind):
    blocks, dimension = real.shape[0], real.shape[-1]
    flat = (dimension, dimension)

    def body(weight, real, partner, imag, ahead, behind, for_partner, own, middle, shared):
        outer = is_at(0, sections)
        chosen = first_is_far()
        for index in range(blocks):
            far = jnp.where(chosen, ahead[index], behind[index])
            near = jnp.where(chosen, behind[index], ahead[index])
            value = imag[index]
            for_partner[index] = weight[NEXT] * value + weight[OTHER] * far
            own[index] = weight[OWN] * value + weight[LONE] * far + weight[PAIR] * near
        last = blocks - 1
        middle[0] = for_partner[last]
        middle[1] = own[last]
        for place, table in enumerate((real, partner, for_partner, own)):
            shared[place] = jnp.where(outer, table[last], table[0])

    def shape(count):
        return jax.ShapeDtypeStruct((count,) + flat, F32)

    return call(
        body,
        (shape(blocks), shape(blocks), shape(2), shape(4)),
        [side_weight, real, partner, imag, ahead, behind],
        1,
    )


def combine(sections, tables, early):
    names = list(tables)
    blocks, dimension = tables["real"].shape[0], tables["real"].shape[-1]
    last = blocks - 1
    count = 1 if early else last

    def body(*refs):
        t = dict(zip(names, refs))
        to_first, to_second, to_partner, own = refs[len(names) :]
        a, b = t["local_weight"], t["side_weight"]
        chosen = first_is_far()

        def emit(place, index, ends):
            sides = []
            for number, name in enumerate(("real", "partner", "side_partner", "side_own")):
                terms = [t[name][i] for i in (index - 1, index + 1) if 0 <= i <= last]
                terms += [end(number) for end in ends]
                sides.append(functools.reduce(jnp.add, terms))
            n_real, n_partner, n_for, n_own = sides
            real, partner, imag = t["real"][index], t["partner"][index], t["imag"][index]
            ahead, behind = t["ahead"][index], t["behind"][index]
            far = jnp.where(chosen, ahead, behind)
            near = jnp.where(chosen, behind, ahead)
            pair = a[PAIR] * real + a[NEXT] * partner + b[PAIR] * n_real + b[NEXT] * n_partner
            lone = a[LONE] * real + b[LONE] * n_real
            to_first[place] = jnp.where(chosen, pair, lone)
            to_second[place] = jnp.where(chosen, lone, pair)
            to_partner[place] = a[NEXT] * imag + a[OTHER] * far + n_for
            own[2 * place] = (
                a[OWN] * real + a[OTHER] * partner + b[OWN] * n_real + b[OTHER] * n_partner
            )
            own[2 * place + 1] = a[OWN] * imag + a[LONE] * far + a[PAIR] * near + n_own

        def middle(number):
            return t["middle_real"][number] if number < 2 else t["middle"][number - 2]

        def shared(number):
            return t["shared"][number]

        outer = is_at(0, sections)

        @pl.when(outer)
        def _():
            for place in range(count):
                index = 0 if early else place + 1
                emit(place, index, [shared] if not early and index == last else [])

        @pl.when(jnp.logical_not(outer))
        def _():
            for place in range(count):
                index = last if early else place
                emit(place, index, [middle] if early else [shared] if index == 0 else [])

    def shape(count):
        return jax.ShapeDtypeStruct((count, dimension, dimension), F32)

    return call(
        body,
        (shape(count), shape(count), shape(count), shape(2 * count)),
        [tables[name] for name in names],
        1,
    )


def finish(sections, blocks, group, early, written):
    own, dimension = group[0], group[0].shape[-1]
    last = blocks - 1
    count = own.shape[0] // 2

    def body(own, from_first, from_second, from_partner, *rest):
        out, total, sems = rest[-3:]
        right_half = half_of(sections)
        outer = is_at(0, sections)
        copies = []
        for k in range(count):
            low, high = (0, last) if early else (k + 1, k)
            index = jnp.where(outer, low, high)
            place = jnp.where(right_half, last - index, index)
            for part in (1, 0):
                slot = 2 * k + part
                if part:
                    total[slot] = own[slot] + from_partner[k]
                else:
                    total[slot] = own[slot] + (from_first[k] + from_second[k])
                copies.append(
                    pltpu.make_async_copy(total.at[slot], out.at[0, place, part], sems.at[slot])
                )
                copies[-1].start()
        for copy in copies:
            copy.wait()

    outside = pl.BlockSpec(memory_space=pltpu.HBM)
    before = [] if written is None else [written]
    return pl.pallas_call(
        body,
        out_shape=jax.ShapeDtypeStruct((1, blocks, 2, dimension, dimension), F32),
        in_specs=[VMEM] * 4 + [outside] * len(before),
        out_specs=outside,
        scratch_shapes=[
            pltpu.VMEM((2 * count, dimension, dimension), F32),
            pltpu.SemaphoreType.DMA((2 * count,)),
        ],
        input_output_aliases={4: 0} if before else {},
        compiler_params=pltpu.CompilerParams(vmem_limit_bytes=12 << 20),
    )(*group, *before)


def chosen_first(sections, outer_value, inner_value):
    return jnp.where(is_at(0, sections), outer_value, inner_value)


def step(
    onsite, hopping, coupling, broadening, born_sigma, phonon_shift, phonon_local, phonon_side
):
    blocks = onsite.shape[0]
    sections = lax.axis_size("section")
    spread = lax.axis_size("energy")
    assert born_sigma.shape[0] == 1 and spread % 2 == 0
    assert sections % 4 == 0 and sections // 4 == 1 and blocks >= 2
    half = sections // 2
    last = blocks - 1
    pairs = [(s, s ^ 1) for s in range(sections)]
    across = [(half - 1, half), (half, half - 1)]

    def over_section(value, route):
        return lax.ppermute(value, "section", route)

    def over_energy(value, route):
        return lax.ppermute(value, "energy", route)

    swap = [(e, e ^ 1) for e in range(spread)]
    first_swap = [(e, e ^ 2) for e in range(spread) if e ^ 2 < spread]
    second_swap = [(e, ((e + 2) ^ 2) - 2) for e in range(spread)]
    second_swap = [(a, b) for a, b in second_swap if 0 <= b < spread]
    crossing = []
    for a, b in swap:
        for s, t in across + [(0, 0), (sections - 1, sections - 1)]:
            crossing.append((a * sections + s, (b if s == t else a) * sections + t))

    pack, begun = prepare(sections, spread, broadening, onsite, hopping, coupling, born_sigma)

    def inner_link(table, index, reverse=False):
        place = 2 * blocks + 2 * index
        return [(table, place + 1, place) if reverse else (table, place, place + 1)]

    end = 4 * blocks - 2

    first = []
    sigma = None
    for step in range(half):
        entering = []
        if step > 0:
            sigma = enter_step(sections, step, 1, pack, sigma)
        for index in range(blocks):
            entering.append(sigma)
            given = [] if sigma is None else [sigma]
            if step == 0 and index == 0:
                sigma = begun
                continue
            leaves = index == last
            link = [(pack, end, end + 1)] if leaves else inner_link(pack, index)
            sigma = chain_step(sections, step, pack, index, given, link, leaves=leaves)
        first.append(entering)
        leaving = sigma
        if step < half - 1:
            sigma = over_section(sigma, pairs)
        else:
            sigma = lax.ppermute(sigma, ("energy", "section"), crossing)

    all_weights = weights(phonon_shift, phonon_local, phonon_side, leaving)
    local_weight, side_weight = all_weights
    pack_in = over_section(pack, pairs)
    arriving = enter_step(sections, half - 1, 0, pack, sigma)
    earlier = tuple(first[step][last] for step in range(half))
    sigma = over_section(arriving, pairs)
    ready = green_step(
        sections, half - 1, pack, last, (first[half - 1][last], arriving), after=all_weights
    )
    for index in range(last, -1, -1):
        link = (
            inner_link(pack_in, index - 1, True)
            if index > 0
            else [(pack, end + 1, end), (pack_in, end, end + 1)]
        )
        after = ready if index == last else ()
        sigma = chain_step(sections, 0, pack_in, index, [sigma], link, after=after)
    entered = (sigma, arriving)
    between = []
    for index in range(last, 0, -1):
        link = inner_link(pack, index - 1, True)
        sent = chain_step(sections, None, pack, index, entered, link, after=ready)
        entered = (sent,)
        if index > 1:
            kept = chosen_first(sections, *(first[step][index - 1] for step in range(half)))
            between.insert(0, green_step(sections, None, pack, index - 1, (kept, sent)))
    real, imag = greens_at_ends(
        sections, pack, (first[0][last], sigma), ready, first[half - 1][0], entered[0], between
    )
    partner = over_energy(real, swap)
    ahead = over_energy(imag, first_swap)
    behind = over_energy(imag, second_swap)
    middle_real = over_section(last_blocks(real, partner), across)

    side_partner, side_own, middle, shared = side_terms(
        sections, side_weight, real, partner, imag, ahead, behind
    )
    middle = over_section(middle, across)
    shared = over_section(shared, pairs)
    tables = {
        "local_weight": local_weight,
        "side_weight": side_weight,
        "real": real,
        "partner": partner,
        "imag": imag,
        "ahead": ahead,
        "behind": behind,
        "side_partner": side_partner,
        "side_own": side_own,
    }

    def exchange(to_first, to_second, to_partner, own):
        from_first = over_energy(to_first, first_swap)
        from_second = over_energy(to_second, second_swap)
        from_partner = over_energy(to_partner, swap)
        return own, from_first, from_second, from_partner

    ends = {"middle_real": middle_real, "middle": middle}
    early = combine(sections, tables | ends, True)
    early = exchange(*early)
    late = combine(sections, tables | {"shared": shared}, False)
    late = exchange(*late)
    result = finish(sections, blocks, early, True, None)
    return finish(sections, blocks, late, False, result)


def solution(mesh):
    in_specs = (
        P("section", None),
        P("section", None, None),
        P("section", None, None),
        P("energy"),
        P("energy", "section", None, None, None),
        P(),
        P(),
        P(),
    )
    out_specs = P("energy", "section", None, None, None)
    return jax.shard_map(step, mesh=mesh, in_specs=in_specs, out_specs=out_specs, check_vma=False)
```
